32 devices in a mesh: tm: 8 (over z, y), emit: 4 (over x, core).
Axes of the slice: x: 2, y: 2, z: 4, core: 2. Of those that a mesh axis runs over, the one named last changes fastest.
Arguments:
- observed: int32 [8, 512], P('emit', 'tm'), may hold values from 0 to 4095
- starts: int32 [8], P('emit'), may hold values from 0 to 255
- initial: float32 [256], replicated, may hold values from 0.1 to 1
- transition: float32 [256, 256], replicated, may hold values from 0 to 1, as said below
- emission: float32 [4096, 256], P('emit'), may hold values from 0.5 to 2
Outputs:
- posterior: float32 [8, 512, 256], P('emit', 'tm')
- new_emission: float32 [4096, 256], P(('tm', 'emit'))
- loglik: float32 [8], P('emit')
The draws below stay inside these ranges and needn't reach their ends.
Inputs may be any that keep to these rules, and one draw needn't show every extreme that they name: `transition`: entries positive.
All inputs are finite; a program needn't handle non-finite values.
Results may differ from the reference program's by a relative error of at most 0.0003.
Values sent between devices are 32-bit elements; how exact they have to be, the bound alone decides.
No kernel may reach another device: no remote copies, remote signals or barrier semaphores. Data moves between devices by JAX's collectives and lax.ppermute only.
A program may use at most 128 MiB of HBM per device.

```python
import math
import jax
import jax.numpy as jnp
from jax import lax

S = 256
M = 4096
LENGTH = 512
TRAJ = 8


def draw_transition(key, part):
    rate_key, mix_key = jax.random.split(jax.random.fold_in(key, 17))
    low_rate = jnp.log(0.1 / LENGTH)
    high_rate = jnp.log(0.05)
    rates = jnp.exp(jax.random.uniform(rate_key, (S, 1), jnp.float32, low_rate, high_rate))
    mixing = jax.random.uniform(mix_key, (S, S), jnp.float32, 0.5, 1.5)
    diagonal = (jnp.arange(S)[:, None] == jnp.arange(S)[None, :]).astype(jnp.float32)
    return (1.0 - rates) * diagonal + rates * mixing / S


def plant(entries, stream_key, least, largest):
    shape = entries.shape
    spot = [jax.random.randint(jax.random.fold_in(stream_key, axis), (), 0, shape[axis]) for axis in range(len(shape))]
    entries = entries.at[tuple(spot)].set(least)
    longest = shape.index(max(shape))
    spot[longest] = (spot[longest] + 1) % shape[longest]
    return entries.at[tuple(spot)].set(largest)


def level_of(own_key, extent, pieces, least, top_value):
    factor_of = 1.0
    for axis_at, shards_of in pieces:
        draws = jax.random.uniform(jax.random.fold_in(jax.random.fold_in(own_key, 6), axis_at), (shards_of,), jnp.float32, least / len(pieces), top_value / len(pieces))
        factor_of = factor_of * jnp.repeat(jnp.exp(draws), extent[axis_at] // shards_of).reshape((-1,) + (1,) * (len(extent) - 1 - axis_at))
    return factor_of


def setup_inputs(seed: int = 0) -> dict:
    arg_keys = jax.random.split(jax.random.key(seed), 6)
    return {
        "observed": plant(jax.random.randint(arg_keys[0], (TRAJ, LENGTH), 0, M), jax.random.fold_in(arg_keys[0], 1), 0, M - 1).astype(jnp.int32),
        "starts": plant(jax.random.randint(arg_keys[1], (TRAJ,), 0, LENGTH // 2), jax.random.fold_in(arg_keys[1], 1), 0, (LENGTH // 2) - 1).astype(jnp.int32),
        "initial": jnp.clip(jnp.exp(jax.random.uniform(arg_keys[2], (S,), jnp.float32, math.log(0.1), math.log(1.0))), 0.1, 1.0),
        "transition": draw_transition(jax.random.fold_in(arg_keys[5], 71), 0),
        "emission": jnp.clip(jnp.exp(math.log(2.0) - 1.3862944 * jax.random.uniform(arg_keys[4], (M, S), jnp.float32) ** level_of(arg_keys[4], (M, S), ((0, 4),), -0.2, 0.2)), 0.5, 2.0),
    }


highest = lax.Precision.HIGHEST
pseudo_count = 0.01


def reference(observed, starts, initial, transition, emission):
    weights = jnp.take(emission, observed, axis=0)
    frame_ids = jnp.arange(LENGTH, dtype=jnp.int32)
    active = frame_ids[None, :] >= starts[:, None]
    prior_state = initial / jnp.sum(initial)
    forward_start = jnp.broadcast_to(prior_state, (observed.shape[0], S))
    weight_seq = jnp.swapaxes(weights, 0, 1)
    active_seq = active.T

    def forward_step(previous, inputs):
        weight_now, active_now = inputs
        moved = jnp.dot(previous, transition, precision=highest) * weight_now
        scaling = jnp.sum(moved, axis=1)
        updated = jnp.where(active_now[:, None], moved / scaling[:, None], previous)
        return updated, (updated, jnp.where(active_now, jnp.log(scaling), jnp.zeros_like(scaling)))

    _, (forward, log_scales) = lax.scan(forward_step, forward_start, (weight_seq, active_seq))

    backward_start = jnp.ones_like(forward_start) / S

    def backward_step(later_msg, inputs):
        weight_now, active_now = inputs
        moved = jnp.dot(later_msg * weight_now, transition.T, precision=highest)
        earlier = jnp.where(active_now[:, None], moved / jnp.sum(moved, axis=1, keepdims=True), later_msg)
        return earlier, later_msg

    _, backward = lax.scan(backward_step, backward_start, (weight_seq, active_seq), reverse=True)
    joint_prob = forward * backward
    occupancy = jnp.where(active_seq[:, :, None], joint_prob / jnp.sum(joint_prob, axis=2, keepdims=True), jnp.zeros_like(joint_prob))
    occupancy = jnp.swapaxes(occupancy, 0, 1)
    posterior = S * occupancy
    counts = jax.ops.segment_sum(occupancy.reshape(-1, S), observed.reshape(-1), num_segments=M)
    totals = jnp.sum(occupancy, axis=(0, 1))
    new_emission = M * (counts + pseudo_count) / (totals + M * pseudo_count)
    loglik = jnp.sum(log_scales, axis=0) / (LENGTH - starts).astype(jnp.float32)
    return posterior, new_emission, loglik
```

```python
import jax
import jax.numpy as jnp
from jax import lax
from jax.experimental import pallas as pl
from jax.experimental.pallas import tpu as pltpu
from jax.sharding import PartitionSpec as P

pseudo_count = 0.01
f32 = jnp.float32
bf16 = jnp.bfloat16
chunks = 8
slots = 16
rows_sent = 14


def split2(x):
    high = x.astype(bf16)
    return high, (x - high.astype(f32)).astype(bf16)


def split3(x):
    high = x.astype(bf16)
    rest = x - high.astype(f32)
    mid = rest.astype(bf16)
    return high, mid, (rest - mid.astype(f32)).astype(bf16)


def iota(shape, dim):
    return lax.broadcasted_iota(jnp.int32, shape, dim)


def dot(a, b):
    return lax.dot_general(a, b, (((1,), (0,)), ((), ())), preferred_element_type=f32)


def dot_nt(a, b):
    return lax.dot_general(a, b, (((1,), (1,)), ((), ())), preferred_element_type=f32)


def stack3(x):
    high = x.astype(bf16).astype(f32)
    rest = x - high
    mid = rest.astype(bf16).astype(f32)
    return jnp.concatenate([high, mid, rest - mid], axis=0).astype(bf16)


def combine(y, rows, states, terms):
    def part(i, j):
        return y[i * rows : (i + 1) * rows, j * states : (j + 1) * states]

    small = part(1, 1) + part(2, 0)
    if terms == 3:
        small = small + part(0, 2)
    return part(0, 0) + ((part(0, 1) + part(1, 0)) + small)


def row_times(x, cat, states, terms):
    return combine(dot(stack3(x), cat), x.shape[0], states, terms)


def times_col(x, cat, states, terms):
    return combine(dot_nt(stack3(x), cat), x.shape[0], states, terms)


def take(ref, start, steps):
    return jnp.concatenate([ref.at[h][pl.ds(start, chunks, stride=steps), :] for h in range(ref.shape[0])], axis=1)


def put(ref, start, steps, x):
    for h in range(ref.shape[0]):
        ref.at[h][pl.ds(start, chunks, stride=steps), :] = x[:, h * 128 : (h + 1) * 128]


def whole(ref):
    return jnp.concatenate([ref[h] for h in range(ref.shape[0])], axis=1)


def normalize(x):
    return x / jnp.sum(x, axis=1, keepdims=True)


def gather_kernel(ids_ref, table_ref, out_ref):
    groups, frames = ids_ref.shape
    rows, states = table_ref.shape
    high, mid, low = split3(table_ref[...])
    eye = iota((frames, frames), 0) == iota((frames, frames), 1)
    lanes = iota((frames, rows), 1)
    for k in range(groups):
        wide = jnp.where(eye, jnp.broadcast_to(ids_ref[k : k + 1, :], (frames, frames)), 0)
        column = jnp.sum(wide, axis=1, keepdims=True)
        pick = jnp.where(column == lanes, 1.0, 0.0).astype(bf16)
        out_ref[k] = dot(pick, high) + (dot(pick, mid) + dot(pick, low))


def product_kernel(scal_ref, own_ref, *refs):
    count = len(refs) - 8
    recv_refs = refs[:count]
    trans_ref, init_ref, w_ref, high_ref, low_ref, state_ref, msg_ref, x_ref = refs[count:]
    frames, states = w_ref.shape
    steps = frames // chunks
    first = scal_ref[0]
    w = own_ref[0]
    for r in recv_refs:
        w = w + r[...]
    w_ref[...] = w
    trans = trans_ref[...]
    t1, t2 = split2(trans)
    eye = jnp.where(iota((states, states), 0) == iota((states, states), 1), 1.0, 0.0)

    def inverse_sum(x):
        return 1.0 / jnp.sum(jnp.sum(x, axis=0, keepdims=True), axis=1, keepdims=True)

    scales = []
    for c in range(chunks):
        x = jnp.where(c * steps >= first, trans * w_ref[c * steps : c * steps + 1, :], eye)
        x_ref[c] = x
        scales.append(inverse_sum(x))

    def step(k, scales):
        after = []
        for c in range(chunks):
            x = x_ref[c] * scales[c]
            x1, x2 = split2(x)
            y = dot(x1, t1) + (dot(x1, t2) + dot(x2, t1))
            y = y * w_ref[pl.ds(c * steps + k, 1), :]
            y = jnp.where(c * steps + k >= first, y, x)
            x_ref[c] = y
            after.append(inverse_sum(y))
        return tuple(after)

    scales = lax.fori_loop(1, steps, step, tuple(scales))
    at = 0
    level = []
    for c in range(chunks):
        x1, x2 = split2(x_ref[c] * scales[c])
        high_ref[at] = x1
        low_ref[at] = x2
        level.append(at)
        at += 1
    while len(level) > 1:
        upper = []
        for i in range(0, len(level), 2):
            a1, a2 = high_ref[level[i]], low_ref[level[i]]
            b1, b2 = high_ref[level[i + 1]], low_ref[level[i + 1]]
            y = dot(a1, b1) + (dot(a1, b2) + dot(a2, b1))
            y1, y2 = split2(y * inverse_sum(y))
            high_ref[at] = y1
            low_ref[at] = y2
            upper.append(at)
            at += 1
        level = upper
    init = init_ref[...]
    prior = jnp.broadcast_to(init / jnp.sum(init, axis=1, keepdims=True), (8, states))
    final = jnp.full((8, states), 1.0 / states, f32)
    root1, root2 = high_ref[level[0]], low_ref[level[0]]
    ahead = row_times(prior, jnp.concatenate([root1, root2], axis=1), states, 2)
    behind = times_col(final, jnp.concatenate([root1, root2], axis=0), states, 2)
    top = iota((8, states), 0) == 0
    state_ref[...] = jnp.where(top, prior, final)
    msg_ref[...] = jnp.where(top, normalize(ahead), normalize(behind))


def merge_state(state, recv, part, parts, turn):
    spot = iota(state.shape, 0)
    take = ((spot == 0) & (part == turn + 1)) | ((spot == 1) & (part == parts - 2 - turn))
    return jnp.where(take, recv, state)


def relay_kernel(parts, turn, scal_ref, state_ref, recv_ref, high_ref, low_ref, out_ref, msg_ref):
    states = state_ref.shape[1]
    state = merge_state(state_ref[...], recv_ref[...], scal_ref[1], parts, turn - 1)
    out_ref[...] = state
    root1, root2 = high_ref[0], low_ref[0]
    ahead = row_times(state, jnp.concatenate([root1, root2], axis=1), states, 2)
    behind = times_col(state, jnp.concatenate([root1, root2], axis=0), states, 2)
    msg_ref[...] = jnp.where(iota((8, states), 0) == 0, normalize(ahead), normalize(behind))


def place(ids_ref, scal_ref, block, turn):
    frames = ids_ref.shape[1]
    square = (frames, frames)
    bits = block.bit_length() - 1
    down, across = iota(square, 0), iota(square, 1)
    row = jnp.broadcast_to(ids_ref[0:1, :], square)
    live = across >= scal_ref[0]
    column = jnp.broadcast_to(jnp.sum(jnp.where(down == across, row, 0), axis=1, keepdims=True), square)
    live_column = down >= scal_ref[0]
    owner_row = jnp.where(live, lax.shift_right_logical(row, bits), -1)
    owner_column = jnp.where(live_column, lax.shift_right_logical(column, bits), -1)
    same = owner_row == owner_column
    rank_row = jnp.sum(jnp.where(same & (down < across), 1, 0), axis=0, keepdims=True)
    rank_column = jnp.sum(jnp.where(same & (across < down), 1, 0), axis=1, keepdims=True)
    most = jnp.max(jnp.where(live[0:1, :], rank_row + 1, 0))
    rank_row = rank_row - rows_sent * turn
    rank_column = rank_column - rows_sent * turn
    fits_row = (rank_row >= 0) & (rank_row < rows_sent) & live[0:1, :]
    fits_column = (rank_column >= 0) & (rank_column < rows_sent) & live_column[:, 0:1]
    local = (column - lax.shift_left(lax.shift_right_logical(column, bits), bits))[:, 0:1]
    return owner_row[0:1, :], rank_row, fits_row, rank_column, fits_column, local, most


def pack(ids_ref, scal_ref, occupancy, send_ref, block, turn, log_sum):
    frames, states = occupancy.shape
    devices = send_ref.shape[0] // slots
    owner, rank, fits, rank_column, fits_column, local, most = place(ids_ref, scal_ref, block, turn)
    spot = jnp.where(fits, owner * slots + rank, -1)
    lines = iota((devices * slots, frames), 0)
    pick = lines == spot
    totals = (lax.bitwise_and(lines, slots - 1) == rows_sent) & (turn == 0)
    pick = jnp.where(pick | totals, 1.0, 0.0).astype(bf16)
    high, mid, low = split3(occupancy)
    base = scal_ref[2]
    lanes = iota((frames, states), 1)
    ranked = jnp.where(fits_column & (lanes == base + rank_column), (local + 1).astype(f32), 0.0).astype(bf16)
    mine = jnp.where((lines == owner * slots + slots - 1) & fits, 1.0, 0.0).astype(bf16)
    sent = dot(pick, high) + (dot(pick, mid) + (dot(pick, low) + dot(mine, ranked)))
    lines = lax.bitwise_and(iota((devices * slots, 1), 0), slots - 1) == slots - 1
    lanes = iota((1, states), 1)
    sent = jnp.where(lines & (lanes == base + rows_sent), log_sum, sent)
    send_ref[...] = jnp.where(lines & (lanes == base + rows_sent + 1), most.astype(f32), sent)


def chain_kernel(parts, block, scal_ref, state_ref, recv_ref, w_ref, high_ref, low_ref, trans_ref, ids_ref,
                 keep_ref, away_ref, occ_ref, send_ref, split_ref, fore_ref, back_ref,
                 start_ref, end_ref, post_ref):
    frames, states = w_ref.shape
    steps = frames // chunks
    first = scal_ref[0]
    state = merge_state(state_ref[...], recv_ref[...], scal_ref[1], parts, parts - 2)
    start_ref[0:1, :] = state[0:1, :]
    end_ref[chunks - 1 : chunks, :] = state[1:2, :]
    width = chunks
    offsets = {}
    at = 0
    size = chunks
    while size >= 1:
        offsets[chunks // size] = at
        at += size
        size //= 2
    while width > 1:
        half = width // 2
        for g in range(chunks // width):
            left = offsets[half] + 2 * g
            lead = jnp.broadcast_to(start_ref[g * width : g * width + 1, :], (8, states))
            cat = jnp.concatenate([high_ref[left], low_ref[left]], axis=1)
            made = normalize(row_times(lead, cat, states, 2))
            start_ref[g * width + half : g * width + half + 1, :] = made[0:1, :]
            last = g * width + width - 1
            tail = jnp.broadcast_to(end_ref[last : last + 1, :], (8, states))
            cat = jnp.concatenate([high_ref[left + 1], low_ref[left + 1]], axis=0)
            made = normalize(times_col(tail, cat, states, 2))
            end_ref[last - half : last - half + 1, :] = made[0:1, :]
        width = half
    trans = trans_ref[...]
    ahead = jnp.concatenate(split3(trans), axis=1)
    behind = jnp.concatenate(split3(trans), axis=0)
    for h in range(states // 128):
        split_ref[h] = w_ref[:, h * 128 : (h + 1) * 128]
    fore = start_ref[...]
    back = end_ref[...]
    logs = jnp.zeros((chunks, 1), f32)
    spots = iota((chunks, 1), 0) * steps
    for k in range(steps):
        moved = row_times(fore, ahead, states, 3) * take(split_ref, k, steps)
        scaling = jnp.sum(moved, axis=1, keepdims=True)
        active = spots + k >= first
        fore = jnp.where(active, moved / scaling, fore)
        logs = logs + jnp.where(active, jnp.log(scaling), 0.0)
        put(fore_ref, k, steps, fore)
        j = steps - 1 - k
        put(back_ref, j, steps, back)
        moved = times_col(back * take(split_ref, j, steps), behind, states, 3)
        back = jnp.where(spots + j >= first, normalize(moved), back)
    joint = whole(fore_ref) * whole(back_ref)
    occupancy = jnp.where(iota((frames, 1), 0) >= first, normalize(joint), 0.0)
    occ_ref[...] = occupancy
    post_ref[...] = states * occupancy
    side = scal_ref[3]
    half = frames // 2
    keep_ref[...] = post_ref[pl.ds(pl.multiple_of(side * half, half), half), :]
    away_ref[...] = post_ref[pl.ds(pl.multiple_of((1 - side) * half, half), half), :]
    pack(ids_ref, scal_ref, occupancy, send_ref, block, 0, jnp.sum(logs))


def counted(recv_ref, block):
    lines, states = recv_ref.shape
    counts = jnp.zeros((block, states), f32)
    totals = jnp.zeros((1, states), f32)
    slot = lax.bitwise_and(iota((block, states), 1), slots - 1)
    line = lax.bitwise_and(iota((states, states), 0), slots - 1)
    row = (iota((block, states), 0) + 1).astype(f32)
    metas = []
    for g in range(lines // states):
        came = recv_ref[g * states : (g + 1) * states, :]
        meta = jnp.sum(jnp.where(line == slots - 1, came, 0.0), axis=0, keepdims=True)
        totals = totals + jnp.sum(jnp.where(line == rows_sent, came, 0.0), axis=0, keepdims=True)
        pick = jnp.where((meta == row) & (slot < rows_sent), 1.0, 0.0).astype(bf16)
        high, mid, low = split3(came)
        counts = counts + (dot(pick, high) + (dot(pick, mid) + dot(pick, low)))
        metas.append(meta)
    return counts, totals, metas


def emit_update(counts, totals, total_rows):
    return total_rows * (counts + pseudo_count) / (totals + total_rows * pseudo_count)


def final_kernel(block, total_rows, emit_count, length, scal_ref, recv_ref, keep_ref, other_ref,
                 post_ref, new_ref, log_ref, counts_ref, totals_ref, most_ref):
    states = recv_ref.shape[1]
    counts, totals, metas = counted(recv_ref, block)
    counts_ref[...] = counts
    totals_ref[...] = totals
    new_ref[...] = emit_update(counts, totals, total_rows)
    lanes = iota((1, states), 1)
    slot = lax.bitwise_and(lanes, slots - 1)
    most = 0.0
    sums = [0.0, 0.0]
    for g, meta in enumerate(metas):
        most = jnp.maximum(most, jnp.max(jnp.where(slot == rows_sent + 1, meta, 0.0)))
        source = g * (states // slots) + lax.shift_right_logical(lanes, slots.bit_length() - 1)
        column = (lax.bitwise_and(source, emit_count - 1) == scal_ref[4]) & (slot == rows_sent)
        odd = lax.bitwise_and(lax.shift_right_logical(source, emit_count.bit_length() - 1), 1)
        for j in range(2):
            sums[j] = sums[j] + jnp.sum(jnp.where(column & (odd == j), meta, 0.0))
    most_ref[0] = most.astype(jnp.int32)
    for j in range(2):
        log_ref[j] = sums[j] / (length - scal_ref[5 + j]).astype(f32)
    side = scal_ref[3]
    post_ref[side] = keep_ref[...]
    post_ref[1 - side] = other_ref[...]


def pack_kernel(block, scal_ref, turn_ref, occ_ref, ids_ref, send_ref):
    pack(ids_ref, scal_ref, occ_ref[...], send_ref, block, turn_ref[0], 0.0)


def more_kernel(block, recv_ref, counts_ref, out_ref):
    counts, _, _ = counted(recv_ref, block)
    out_ref[...] = counts_ref[...] + counts


vmem = pl.BlockSpec(memory_space=pltpu.MemorySpace.VMEM)
smem = pl.BlockSpec(memory_space=pltpu.MemorySpace.SMEM)


def call(kernel, name, in_specs, out_specs, out_shape, scratch=()):
    return pl.pallas_call(kernel, name=name, in_specs=in_specs, out_specs=out_specs, out_shape=out_shape,
                          scratch_shapes=scratch)


def shape(*dims, dtype=f32):
    return jax.ShapeDtypeStruct(dims, dtype)


def shards(observed, starts, initial, transition, emission):
    traj_rows, frame_count = observed.shape
    states = transition.shape[0]
    tm_count = lax.axis_size("tm")
    tm_place = lax.axis_index("tm")
    emit_count = lax.axis_size("emit")
    emit_place = lax.axis_index("emit")
    both = ("tm", "emit")
    devices = tm_count * emit_count
    own_rows = emission.shape[0]
    total_rows = own_rows * emit_count
    block = total_rows // devices
    length = frame_count * tm_count
    assert traj_rows == 2 and tm_count % 2 == 0
    frames = 2 * frame_count
    parts = tm_count // 2
    part = tm_place // 2
    side = tm_place % 2
    flat = tm_place * emit_count + emit_place

    kept = jnp.where(side == 0, observed[0:1], observed[1:2])
    given = jnp.where(side == 0, observed[1:2], observed[0:1])
    taken = lax.ppermute(given, "tm", [(i, i ^ 1) for i in range(tm_count)])
    ids = jnp.where(side == 0, jnp.concatenate([kept, taken], axis=1), jnp.concatenate([taken, kept], axis=1))
    first = jnp.where(side == 0, starts[0], starts[1]) - part * frames
    scal = jnp.stack([first, part, (flat % (states // slots)) * slots, side, emit_place, starts[0], starts[1]])
    scal = scal.astype(jnp.int32)

    def swaps(k):
        return [(i, i ^ k) for i in range(emit_count)]

    others = [lax.ppermute(ids, "emit", swaps(k)) for k in range(1, emit_count)]
    wanted = jnp.concatenate([ids] + others, axis=0) - emit_place * own_rows
    rows = call(gather_kernel, "gather", [vmem, vmem], vmem, shape(emit_count, frames, states))(wanted, emission)
    came = [lax.ppermute(rows[k], "emit", swaps(k)) for k in range(1, emit_count)]
    nodes = 2 * chunks - 1
    weights, high, low, state, message = pl.pallas_call(
        product_kernel, name="product", grid=(1,),
        in_specs=[smem, pl.BlockSpec((1, frames, states), lambda i: (0, 0, 0))]
        + [pl.BlockSpec((frames, states), lambda i: (0, 0))] * (emit_count - 1)
        + [pl.BlockSpec((states, states), lambda i: (0, 0)), pl.BlockSpec((1, states), lambda i: (0, 0))],
        out_specs=[vmem] * 5,
        out_shape=[shape(frames, states), shape(nodes, states, states, dtype=bf16),
                   shape(nodes, states, states, dtype=bf16), shape(8, states), shape(8, states)],
        scratch_shapes=[pltpu.VMEM((chunks, states, states), f32)],
    )(scal, rows, *came, transition, initial.reshape(1, states))

    def relay_pairs(turn):
        pairs = []
        for y in range(2):
            pairs.append((2 * turn + y, 2 * turn + 2 + y))
            pairs.append((2 * (parts - 1 - turn) + y, 2 * (parts - 2 - turn) + y))
        return pairs

    root = pl.BlockSpec((1, states, states), lambda i: (nodes - 1, 0, 0))
    line = pl.BlockSpec((8, states), lambda i: (0, 0))
    recv = lax.ppermute(message, "tm", relay_pairs(0))
    for turn in range(1, parts - 1):
        def relay(*refs, turn=turn):
            relay_kernel(parts, turn, *refs)

        state, message = pl.pallas_call(
            relay, name="relay", grid=(1,), in_specs=[smem, line, line, root, root],
            out_specs=[vmem, vmem], out_shape=[shape(8, states), shape(8, states)],
        )(scal, state, recv, high, low)
        recv = lax.ppermute(message, "tm", relay_pairs(turn))

    def chain(*refs):
        chain_kernel(parts, block, *refs)

    keep, away, occupancy, send = call(
        chain, "chain", [smem] + [vmem] * 7, [vmem] * 4,
        [shape(frame_count, states), shape(frame_count, states), shape(frames, states), shape(devices * slots, states)],
        [pltpu.VMEM((states // 128, frames, 128), f32)] * 3
        + [pltpu.VMEM((chunks, states), f32)] * 2 + [pltpu.VMEM((frames, states), f32)],
    )(scal, state, recv, weights, high, low, transition, ids)
    other = lax.ppermute(away, "tm", [(i, i ^ 1) for i in range(tm_count)])

    def exchange(sent):
        got = lax.all_to_all(sent.reshape(devices, slots, states), both, 0, 0, tiled=True)
        return got.reshape(devices * slots, states)

    def final(*refs):
        final_kernel(block, total_rows, emit_count, length, *refs)

    posterior, new_emission, loglik, counts, totals, most = call(
        final, "final", [smem, vmem, vmem, vmem], [vmem, vmem, smem, vmem, vmem, smem],
        [shape(2, frame_count, states), shape(block, states), shape(2), shape(block, states), shape(1, states),
         shape(1, dtype=jnp.int32)],
    )(scal, exchange(send), keep, other)

    def another(carried):
        turn, counts, _ = carried

        def packs(*refs):
            pack_kernel(block, *refs)

        def more(*refs):
            more_kernel(block, *refs)

        sent = call(packs, "pack", [smem, smem, vmem, vmem], vmem, shape(devices * slots, states))(
            scal, turn.reshape(1), occupancy, ids
        )
        counts = call(more, "more", [vmem, vmem], vmem, shape(block, states))(exchange(sent), counts)
        return turn + 1, counts, emit_update(counts, totals, total_rows)

    _, _, new_emission = lax.while_loop(
        lambda carried: carried[0] * rows_sent < most[0], another, (jnp.int32(1), counts, new_emission)
    )
    return (posterior, new_emission, loglik)


def solution(mesh):
    in_specs = (P("emit", "tm"), P("emit"), P(), P(), P("emit", None))
    out_specs = (P("emit", "tm", None), P(("tm", "emit"), None), P("emit"))
    return jax.shard_map(shards, mesh=mesh, in_specs=in_specs, out_specs=out_specs, check_vma=False)
```

```python
import jax
import jax.numpy as jnp
from jax import lax
from jax.experimental import pallas as pl
from jax.experimental.pallas import tpu as pltpu
from jax.sharding import PartitionSpec as P

pseudo_count = 0.01
f32 = jnp.float32
bf16 = jnp.bfloat16
chunks = 8
slots = 16
rows_sent = 14
granted = 24 << 20


def split2(x):
    high = x.astype(bf16)
    return high, (x - high.astype(f32)).astype(bf16)


def split3(x):
    high = x.astype(bf16)
    rest = x - high.astype(f32)
    mid = rest.astype(bf16)
    return high, mid, (rest - mid.astype(f32)).astype(bf16)


def iota(shape, dim):
    return lax.broadcasted_iota(jnp.int32, shape, dim)


def dot(a, b):
    return lax.dot_general(a, b, (((1,), (0,)), ((), ())), preferred_element_type=f32)


def dot_nt(a, b):
    return lax.dot_general(a, b, (((1,), (1,)), ((), ())), preferred_element_type=f32)


def stack3(x):
    high = x.astype(bf16).astype(f32)
    rest = x - high
    mid = rest.astype(bf16).astype(f32)
    return jnp.concatenate([high, mid, rest - mid], axis=0).astype(bf16)


def combine(y, rows, states, terms):
    def part(i, j):
        return y[i * rows : (i + 1) * rows, j * states : (j + 1) * states]

    small = part(1, 1) + part(2, 0)
    if terms == 3:
        small = small + part(0, 2)
    return part(0, 0) + ((part(0, 1) + part(1, 0)) + small)


def row_times(x, cat, states, terms):
    return combine(dot(stack3(x), cat), x.shape[0], states, terms)


def times_col(x, cat, states, terms):
    return combine(dot_nt(stack3(x), cat), x.shape[0], states, terms)


def take(ref, start, steps):
    return jnp.concatenate([ref.at[h][pl.ds(start, chunks, stride=steps), :] for h in range(ref.shape[0])], axis=1)


def put(ref, start, steps, x):
    for h in range(ref.shape[0]):
        ref.at[h][pl.ds(start, chunks, stride=steps), :] = x[:, h * 128 : (h + 1) * 128]


def whole(ref):
    return jnp.concatenate([ref[h] for h in range(ref.shape[0])], axis=1)


def normalize(x):
    return x / jnp.sum(x, axis=1, keepdims=True)


def diagonal(x):
    return jnp.sum(jnp.where(iota(x.shape, 0) == iota(x.shape, 1), x, 0.0), axis=0, keepdims=True)


def prepare_kernel(table_ref, trans_ref, table1_ref, table2_ref, table3_ref, trans1_ref, trans2_ref, trans3_ref,
                   exact_ref, sums_ref):
    table1_ref[...], table2_ref[...], table3_ref[...] = split3(table_ref[...])
    trans = trans_ref[...]
    t1, t2, t3 = split3(trans)
    trans1_ref[...], trans2_ref[...], trans3_ref[...] = t1, t2, t3
    exact_ref[...] = diagonal(trans) / diagonal(t1.astype(f32) + t2.astype(f32))
    sums_ref[...] = jnp.sum(trans, axis=0, keepdims=True)


def gather_kernel(ids_ref, high_ref, mid_ref, low_ref, mine_ref, other_ref):
    groups, frames = ids_ref.shape
    rows = high_ref.shape[0]
    eye = iota((frames, frames), 0) == iota((frames, frames), 1)
    lanes = iota((frames, rows), 1)
    for k in range(groups):
        wide = jnp.where(eye, jnp.broadcast_to(ids_ref[k : k + 1, :], (frames, frames)), 0)
        column = jnp.sum(wide, axis=1, keepdims=True)
        pick = jnp.where(column == lanes, 1.0, 0.0).astype(bf16)
        taken = dot(pick, high_ref[...]) + (dot(pick, mid_ref[...]) + dot(pick, low_ref[...]))
        (other_ref if k % 2 else mine_ref)[k // 2] = taken


def product_kernel(scal_ref, own_ref, recv_ref, trans_ref, trans1_ref, trans2_ref, trans3_ref, exact_ref, sums_ref,
                   init_ref, w_ref, lead_ref, high_ref, low_ref, state_ref, msg_ref, scaled_ref, column_ref):
    frames, states = w_ref.shape
    steps = frames // chunks
    first = scal_ref[0]
    w_ref[...] = own_ref[...] + recv_ref[...]
    cat = jnp.concatenate([trans1_ref[...], trans2_ref[...], trans3_ref[...]], axis=0)
    lead_ref[...] = times_col(w_ref[...], cat, states, 3)

    def store(c, y, columns):
        column_ref[c : c + 1, :] = columns
        high_ref[c], low_ref[c] = split2(y)

    def reset(c):
        eye = iota((states, states), 0) == iota((states, states), 1)
        high_ref[c] = jnp.where(eye, 1.0, 0.0).astype(bf16)
        low_ref[c] = jnp.zeros((states, states), bf16)
        column_ref[pl.ds(c, 1), :] = jnp.ones((1, states), f32)

    for c in range(chunks):
        row = w_ref[c * steps : c * steps + 1, :]
        row = row / jnp.sum(sums_ref[...] * row, axis=1, keepdims=True)
        store(c, trans_ref[...] * row, sums_ref[...] * row)
    start_chunk = lax.div(first, steps)
    start_step = lax.rem(first, steps)

    def step(k, carried):
        @pl.when((start_step == k) & (first >= 0) & (first < frames))
        def _():
            reset(start_chunk)

        for c in range(chunks):
            frame = c * steps + k
            total = jnp.sum(lead_ref[pl.ds(frame, 1), :] * column_ref[c : c + 1, :], axis=1, keepdims=True)
            scaled_ref[c : c + 1, :] = w_ref[pl.ds(frame, 1), :] * exact_ref[...] / total
        for c in range(chunks):
            x1, x2 = high_ref[c], low_ref[c]
            y = dot(x1, trans1_ref[...]) + (dot(x1, trans2_ref[...]) + dot(x2, trans1_ref[...]))
            y = y * scaled_ref[c : c + 1, :]
            store(c, y, jnp.sum(y, axis=0, keepdims=True))
        return carried

    lax.fori_loop(1, steps, step, 0)
    for c in range(chunks):

        @pl.when((c + 1) * steps <= first)
        def _():
            reset(c)

    def inverse_sum(x):
        return 1.0 / jnp.sum(jnp.sum(x, axis=0, keepdims=True), axis=1, keepdims=True)

    at = chunks
    level = list(range(chunks))
    while len(level) > 1:
        above = []
        for i in range(0, len(level), 2):
            a1, a2 = high_ref[level[i]], low_ref[level[i]]
            b1, b2 = high_ref[level[i + 1]], low_ref[level[i + 1]]
            y = dot(a1, b1) + (dot(a1, b2) + dot(a2, b1))
            high_ref[at], low_ref[at] = split2(y * inverse_sum(y))
            above.append(at)
            at += 1
        level = above
    init = init_ref[...]
    prior = jnp.broadcast_to(init / jnp.sum(init, axis=1, keepdims=True), (8, states))
    final = jnp.full((8, states), 1.0 / states, f32)
    state_ref[...] = jnp.where(iota((8, states), 0) == 0, prior, final)
    carry_over(prior, final, high_ref, low_ref, msg_ref)


def carry_over(fore, back, high_ref, low_ref, msg_ref):
    states = fore.shape[1]
    root1, root2 = high_ref[2 * chunks - 2], low_ref[2 * chunks - 2]
    ahead = row_times(fore, jnp.concatenate([root1, root2], axis=1), states, 2)
    behind = times_col(back, jnp.concatenate([root1, root2], axis=0), states, 2)
    msg_ref[...] = jnp.where(iota((8, states), 0) == 0, normalize(ahead), normalize(behind))


def merge_state(state, recv, part, parts, turn):
    spot = iota(state.shape, 0)
    take = ((spot == 0) & (part == turn + 1)) | ((spot == 1) & (part == parts - 2 - turn))
    return jnp.where(take, recv, state)


def relay_kernel(parts, turn, scal_ref, state_ref, recv_ref, high_ref, low_ref, out_ref, msg_ref):
    state = merge_state(state_ref[...], recv_ref[...], scal_ref[1], parts, turn - 1)
    out_ref[...] = state
    carry_over(state, state, high_ref, low_ref, msg_ref)


def place(ids_ref, scal_ref, block, turn):
    frames = ids_ref.shape[1]
    square = (frames, frames)
    bits = block.bit_length() - 1
    down, across = iota(square, 0), iota(square, 1)
    row = jnp.broadcast_to(ids_ref[0:1, :], square)
    live = across >= scal_ref[0]
    column = jnp.broadcast_to(jnp.sum(jnp.where(down == across, row, 0), axis=1, keepdims=True), square)
    live_column = down >= scal_ref[0]
    owner_row = jnp.where(live, lax.shift_right_logical(row, bits), -1)
    owner_column = jnp.where(live_column, lax.shift_right_logical(column, bits), -1)
    same = owner_row == owner_column
    rank_row = jnp.sum(jnp.where(same & (down < across), 1, 0), axis=0, keepdims=True)
    rank_column = jnp.sum(jnp.where(same & (across < down), 1, 0), axis=1, keepdims=True)
    most = jnp.max(jnp.where(live[0:1, :], rank_row + 1, 0))
    rank_row = rank_row - rows_sent * turn
    rank_column = rank_column - rows_sent * turn
    fits_row = (rank_row >= 0) & (rank_row < rows_sent) & live[0:1, :]
    fits_column = (rank_column >= 0) & (rank_column < rows_sent) & live_column[:, 0:1]
    local = (column - lax.shift_left(lax.shift_right_logical(column, bits), bits))[:, 0:1]
    return owner_row[0:1, :], rank_row, fits_row, rank_column, fits_column, local, most


def address_kernel(block, scal_ref, turn_ref, ids_ref, pick_ref, meta_ref):
    frames = ids_ref.shape[1]
    lines, states = meta_ref.shape
    turn = turn_ref[0]
    owner, rank, fits, rank_column, fits_column, local, most = place(ids_ref, scal_ref, block, turn)
    spot = jnp.where(fits, owner * slots + rank, -1)
    across = iota((lines, frames), 0)
    totals = (lax.bitwise_and(across, slots - 1) == rows_sent) & (turn == 0)
    pick_ref[...] = jnp.where((across == spot) | totals, 1.0, 0.0).astype(bf16)
    base = scal_ref[2]
    lanes = iota((frames, states), 1)
    ranked = jnp.where(fits_column & (lanes == base + rank_column), (local + 1).astype(f32), 0.0).astype(bf16)
    mine = jnp.where((across == owner * slots + slots - 1) & fits, 1.0, 0.0).astype(bf16)
    last = lax.bitwise_and(iota((lines, 1), 0), slots - 1) == slots - 1
    lanes = iota((1, states), 1)
    meta_ref[...] = jnp.where(last & (lanes == base + rows_sent + 1), most.astype(f32), dot(mine, ranked))


def pack(pick_ref, meta_ref, occupancy, send_ref, base, log_sum):
    high, mid, low = split3(occupancy)
    pick = pick_ref[...]
    lines, states = meta_ref.shape
    last = lax.bitwise_and(iota((lines, 1), 0), slots - 1) == slots - 1
    meta = jnp.where(last & (iota((1, states), 1) == base + rows_sent), log_sum, meta_ref[...])
    send_ref[...] = dot(pick, high) + (dot(pick, mid) + (dot(pick, low) + meta))


def chain_kernel(parts, scal_ref, state_ref, recv_ref, w_ref, lead_ref, high_ref, low_ref, trans1_ref,
                 trans2_ref, exact_ref, sums_ref, pick_ref, meta_ref,
                 keep_ref, away_ref, occ_ref, send_ref, split_ref, leads_ref, fore_ref,
                 back_ref, start_ref, end_ref, post_ref):
    frames, states = w_ref.shape
    steps = frames // chunks
    first = scal_ref[0]
    state = merge_state(state_ref[...], recv_ref[...], scal_ref[1], parts, parts - 2)
    start_ref[0:1, :] = state[0:1, :]
    end_ref[chunks - 1 : chunks, :] = state[1:2, :]
    width = chunks
    offsets = {}
    at = 0
    size = chunks
    while size >= 1:
        offsets[chunks // size] = at
        at += size
        size //= 2
    while width > 1:
        half = width // 2
        for g in range(chunks // width):
            left = offsets[half] + 2 * g
            lead = jnp.broadcast_to(start_ref[g * width : g * width + 1, :], (8, states))
            cat = jnp.concatenate([high_ref[left], low_ref[left]], axis=1)
            made = normalize(row_times(lead, cat, states, 2))
            start_ref[g * width + half : g * width + half + 1, :] = made[0:1, :]
            last = g * width + width - 1
            tail = jnp.broadcast_to(end_ref[last : last + 1, :], (8, states))
            cat = jnp.concatenate([high_ref[left + 1], low_ref[left + 1]], axis=0)
            made = normalize(times_col(tail, cat, states, 2))
            end_ref[last - half : last - half + 1, :] = made[0:1, :]
        width = half
    ahead = jnp.concatenate([trans1_ref[...], trans2_ref[...]], axis=1)
    behind = jnp.concatenate([trans1_ref[...], trans2_ref[...]], axis=0)
    exact = exact_ref[...]
    sums = sums_ref[...]
    for h in range(states // 128):
        split_ref[h] = w_ref[:, h * 128 : (h + 1) * 128]
        leads_ref[h] = lead_ref[:, h * 128 : (h + 1) * 128]
    fore = start_ref[...]
    back = end_ref[...]
    logs = jnp.zeros((chunks, 1), f32)
    spots = iota((chunks, 1), 0) * steps
    for k in range(steps):
        scaling = jnp.sum(fore * take(leads_ref, k, steps), axis=1, keepdims=True)
        scaled = take(split_ref, k, steps) * (exact / scaling)
        active = spots + k >= first
        fore = jnp.where(active, row_times(fore, ahead, states, 2) * scaled, fore)
        logs = logs + jnp.where(active, jnp.log(scaling), 0.0)
        put(fore_ref, k, steps, fore)
        j = steps - 1 - k
        put(back_ref, j, steps, back)
        weighed = back * take(split_ref, j, steps)
        inverse = exact / jnp.sum(weighed * sums, axis=1, keepdims=True)
        back = jnp.where(spots + j >= first, times_col(weighed, behind, states, 2) * inverse, back)
    joint = whole(fore_ref) * whole(back_ref)
    occupancy = jnp.where(iota((frames, 1), 0) >= first, normalize(joint), 0.0)
    occ_ref[...] = occupancy
    post_ref[...] = states * occupancy
    side = scal_ref[3]
    half = frames // 2
    keep_ref[...] = post_ref[pl.ds(pl.multiple_of(side * half, half), half), :]
    away_ref[...] = post_ref[pl.ds(pl.multiple_of((1 - side) * half, half), half), :]
    pack(pick_ref, meta_ref, occupancy, send_ref, scal_ref[2], jnp.sum(logs, axis=0, keepdims=True))


def counted(recv_ref, block):
    lines, states = recv_ref.shape
    counts = jnp.zeros((block, states), f32)
    totals = jnp.zeros((1, states), f32)
    slot = lax.bitwise_and(iota((block, states), 1), slots - 1)
    line = lax.bitwise_and(iota((states, states), 0), slots - 1)
    row = (iota((block, states), 0) + 1).astype(f32)
    metas = []
    for g in range(lines // states):
        came = recv_ref[g * states : (g + 1) * states, :]
        meta = jnp.sum(jnp.where(line == slots - 1, came, 0.0), axis=0, keepdims=True)
        totals = totals + jnp.sum(jnp.where(line == rows_sent, came, 0.0), axis=0, keepdims=True)
        pick = jnp.where((meta == row) & (slot < rows_sent), 1.0, 0.0).astype(bf16)
        high, mid, low = split3(came)
        counts = counts + (dot(pick, high) + (dot(pick, mid) + dot(pick, low)))
        metas.append(meta)
    return counts, totals, metas


def emit_update(counts, totals, total_rows):
    return total_rows * (counts + pseudo_count) / (totals + total_rows * pseudo_count)


def final_kernel(block, total_rows, emit_count, length, scal_ref, recv_ref, keep_ref, other_ref,
                 post_ref, new_ref, log_ref, counts_ref, totals_ref, most_ref):
    states = recv_ref.shape[1]
    counts, totals, metas = counted(recv_ref, block)
    counts_ref[...] = counts
    totals_ref[...] = totals
    new_ref[...] = emit_update(counts, totals, total_rows)
    lanes = iota((1, states), 1)
    slot = lax.bitwise_and(lanes, slots - 1)
    most = 0.0
    sums = [0.0, 0.0]
    for g, meta in enumerate(metas):
        most = jnp.maximum(most, jnp.max(jnp.where(slot == rows_sent + 1, meta, 0.0)))
        source = g * (states // slots) + lax.shift_right_logical(lanes, slots.bit_length() - 1)
        column = (lax.bitwise_and(source, emit_count - 1) == scal_ref[4]) & (slot == rows_sent)
        odd = lax.bitwise_and(lax.shift_right_logical(source, emit_count.bit_length() - 1), 1)
        for j in range(2):
            sums[j] = sums[j] + jnp.sum(jnp.where(column & (odd == j), meta, 0.0))
    most_ref[0] = most.astype(jnp.int32)
    for j in range(2):
        log_ref[j] = sums[j] / (length - scal_ref[5 + j]).astype(f32)
    side = scal_ref[3]
    post_ref[side] = keep_ref[...]
    post_ref[1 - side] = other_ref[...]


def pack_kernel(scal_ref, pick_ref, meta_ref, occ_ref, send_ref):
    pack(pick_ref, meta_ref, occ_ref[...], send_ref, scal_ref[2], 0.0)


def more_kernel(block, recv_ref, counts_ref, out_ref):
    counts, _, _ = counted(recv_ref, block)
    out_ref[...] = counts_ref[...] + counts


vmem = pl.BlockSpec(memory_space=pltpu.MemorySpace.VMEM)
smem = pl.BlockSpec(memory_space=pltpu.MemorySpace.SMEM)


def call(kernel, name, in_specs, out_specs, out_shape, scratch=(), cost=None):
    if cost is not None:
        cost = pl.CostEstimate(flops=cost, bytes_accessed=cost // 100, transcendentals=0)
    return pl.pallas_call(kernel, name=name, cost_estimate=cost, in_specs=in_specs, out_specs=out_specs, out_shape=out_shape,
                          scratch_shapes=scratch, compiler_params=pltpu.CompilerParams(vmem_limit_bytes=granted))


def shape(*dims, dtype=f32):
    return jax.ShapeDtypeStruct(dims, dtype)


def shards(observed, starts, initial, transition, emission):
    traj_rows, frame_count = observed.shape
    states = transition.shape[0]
    tm_count = lax.axis_size("tm")
    tm_place = lax.axis_index("tm")
    emit_count = lax.axis_size("emit")
    emit_place = lax.axis_index("emit")
    both = ("tm", "emit")
    devices = tm_count * emit_count
    own_rows = emission.shape[0]
    total_rows = own_rows * emit_count
    block = total_rows // devices
    length = frame_count * tm_count
    assert traj_rows == 2 and tm_count % 2 == 0
    frames = 2 * frame_count
    parts = tm_count // 2
    part = tm_place // 2
    side = tm_place % 2
    flat = tm_place * emit_count + emit_place

    kept = jnp.where(side == 0, observed[0:1], observed[1:2])
    given = jnp.where(side == 0, observed[1:2], observed[0:1])
    taken = lax.ppermute(given, "tm", [(i, i ^ 1) for i in range(tm_count)])
    ids = jnp.where(side == 0, jnp.concatenate([kept, taken], axis=1), jnp.concatenate([taken, kept], axis=1))
    first = jnp.where(side == 0, starts[0], starts[1]) - part * frames
    scal = jnp.stack([first, part, (flat % (states // slots)) * slots, side, emit_place, starts[0], starts[1]])
    scal = scal.astype(jnp.int32)

    def swaps(k):
        return [(i, i ^ k) for i in range(emit_count)]

    narrow = shape(states, states, dtype=bf16)
    table = shape(own_rows, states, dtype=bf16)
    prepared = call(prepare_kernel, "prepare", [vmem] * 2, [vmem] * 8,
                    [table] * 3 + [narrow] * 3 + [shape(1, states)] * 2, cost=400_000_000)(emission, transition)
    tables, matrices, exact, sums = prepared[:3], prepared[3:6], prepared[6], prepared[7]
    near = jnp.concatenate([ids, lax.ppermute(ids, "emit", swaps(1))], axis=0)
    far = [lax.ppermute(near, "emit", swaps(k)) for k in range(2, emit_count, 2)]
    wanted = jnp.concatenate([near] + far, axis=0) - emit_place * own_rows
    half = shape(emit_count // 2, frames, states)
    mine, other = call(gather_kernel, "gather", [vmem] * 4, [vmem, vmem], [half, half])(wanted, *tables)
    both_cores = mine + lax.ppermute(other, "emit", swaps(1))
    came = [lax.ppermute(both_cores[k // 2], "emit", swaps(k)) for k in range(2, emit_count, 2)]
    came = sum(came[1:], came[0])
    nodes = 2 * chunks - 1
    weights, lead, high, low, state, message = call(
        product_kernel, "product", [smem] + [vmem] * 9, [vmem] * 6,
        [shape(frames, states), shape(frames, states), shape(nodes, states, states, dtype=bf16),
         shape(nodes, states, states, dtype=bf16), shape(8, states), shape(8, states)],
        [pltpu.VMEM((chunks, states), f32)] * 2,
    )(scal, both_cores[0], came, transition, *matrices, exact, sums, initial.reshape(1, states))

    def address(turn):
        def kernel(*refs):
            address_kernel(block, *refs)

        lines = devices * slots
        return call(kernel, "address", [smem, smem, vmem], [vmem, vmem],
                    [shape(lines, frames, dtype=bf16), shape(lines, states)], cost=400_000_000)(scal, turn, ids)

    pick, meta = address(jnp.zeros((1,), jnp.int32))

    def relay_pairs(turn):
        pairs = []
        for y in range(2):
            pairs.append((2 * turn + y, 2 * turn + 2 + y))
            pairs.append((2 * (parts - 1 - turn) + y, 2 * (parts - 2 - turn) + y))
        return pairs

    recv = lax.ppermute(message, "tm", relay_pairs(0))
    for turn in range(1, parts - 1):
        def relay(*refs, turn=turn):
            relay_kernel(parts, turn, *refs)

        state, message = call(
            relay, "relay", [smem] + [vmem] * 4, [vmem] * 2, [shape(8, states), shape(8, states)]
        )(scal, state, recv, high, low)
        recv = lax.ppermute(message, "tm", relay_pairs(turn))

    def chain(*refs):
        chain_kernel(parts, *refs)

    keep, away, occupancy, send = call(
        chain, "chain", [smem] + [vmem] * 12, [vmem] * 4,
        [shape(frame_count, states), shape(frame_count, states), shape(frames, states), shape(devices * slots, states)],
        [pltpu.VMEM((states // 128, frames, 128), f32)] * 4
        + [pltpu.VMEM((chunks, states), f32)] * 2 + [pltpu.VMEM((frames, states), f32)],
    )(scal, state, recv, weights, lead, high, low, matrices[0], matrices[1], exact, sums, pick, meta)
    other = lax.ppermute(away, "tm", [(i, i ^ 1) for i in range(tm_count)])

    def exchange(sent):
        got = lax.all_to_all(sent.reshape(devices, slots, states), both, 0, 0, tiled=True)
        return got.reshape(devices * slots, states)

    def final(*refs):
        final_kernel(block, total_rows, emit_count, length, *refs)

    posterior, new_emission, loglik, counts, totals, most = call(
        final, "final", [smem, vmem, vmem, vmem], [vmem, vmem, smem, vmem, vmem, smem],
        [shape(2, frame_count, states), shape(block, states), shape(2), shape(block, states), shape(1, states),
         shape(1, dtype=jnp.int32)],
    )(scal, exchange(send), keep, other)

    def another(carried):
        turn, counts, _ = carried

        def more(*refs):
            more_kernel(block, *refs)

        sent = call(pack_kernel, "pack", [smem] + [vmem] * 3, vmem, shape(devices * slots, states))(
            scal, *address(turn.reshape(1)), occupancy
        )
        counts = call(more, "more", [vmem, vmem], vmem, shape(block, states))(exchange(sent), counts)
        return turn + 1, counts, emit_update(counts, totals, total_rows)

    _, _, new_emission = lax.while_loop(
        lambda carried: carried[0] * rows_sent < most[0], another, (jnp.int32(1), counts, new_emission)
    )
    return (posterior, new_emission, loglik)


def solution(mesh):
    in_specs = (P("emit", "tm"), P("emit"), P(), P(), P("emit", None))
    out_specs = (P("emit", "tm", None), P(("tm", "emit"), None), P("emit"))
    return jax.shard_map(shards, mesh=mesh, in_specs=in_specs, out_specs=out_specs, check_vma=False)
```

```python
import jax
import jax.numpy as jnp
from jax import lax
from jax.experimental import pallas as pl
from jax.experimental.pallas import tpu as pltpu
from jax.sharding import PartitionSpec as P

pseudo_count = 0.01
f32 = jnp.float32
bf16 = jnp.bfloat16
chunks = 8
slots = 16
rows_sent = 14
granted = 24 << 20


def split2(x):
    high = x.astype(bf16)
    return high, (x - high.astype(f32)).astype(bf16)


def split3(x):
    high = x.astype(bf16)
    rest = x - high.astype(f32)
    mid = rest.astype(bf16)
    return high, mid, (rest - mid.astype(f32)).astype(bf16)


def iota(shape, dim):
    return lax.broadcasted_iota(jnp.int32, shape, dim)


def dot(a, b):
    return lax.dot_general(a, b, (((1,), (0,)), ((), ())), preferred_element_type=f32)


def dot_nt(a, b):
    return lax.dot_general(a, b, (((1,), (1,)), ((), ())), preferred_element_type=f32)


def stack3(x):
    high = x.astype(bf16).astype(f32)
    rest = x - high
    mid = rest.astype(bf16).astype(f32)
    return jnp.concatenate([high, mid, rest - mid], axis=0).astype(bf16)


def combine(y, rows, states, terms):
    def part(i, j):
        return y[i * rows : (i + 1) * rows, j * states : (j + 1) * states]

    small = part(1, 1) + part(2, 0)
    if terms == 3:
        small = small + part(0, 2)
    return part(0, 0) + ((part(0, 1) + part(1, 0)) + small)


def row_times(x, cat, states, terms):
    return combine(dot(stack3(x), cat), x.shape[0], states, terms)


def times_col(x, cat, states, terms):
    return combine(dot_nt(stack3(x), cat), x.shape[0], states, terms)


def take(ref, start, steps):
    return jnp.concatenate([ref.at[h][pl.ds(start, chunks, stride=steps), :] for h in range(ref.shape[0])], axis=1)


def put(ref, start, steps, x):
    for h in range(ref.shape[0]):
        ref.at[h][pl.ds(start, chunks, stride=steps), :] = x[:, h * 128 : (h + 1) * 128]


def whole(ref):
    return jnp.concatenate([ref[h] for h in range(ref.shape[0])], axis=1)


def normalize(x):
    return x / jnp.sum(x, axis=1, keepdims=True)


def diagonal(x):
    return jnp.sum(jnp.where(iota(x.shape, 0) == iota(x.shape, 1), x, 0.0), axis=0, keepdims=True)


def table_kernel(table_ref, table1_ref, table2_ref, table3_ref):
    table1_ref[...], table2_ref[...], table3_ref[...] = split3(table_ref[...])


def matrix_kernel(trans_ref, trans1_ref, trans2_ref, trans3_ref, exact_ref, sums_ref):
    trans = trans_ref[...]
    t1, t2, t3 = split3(trans)
    trans1_ref[...], trans2_ref[...], trans3_ref[...] = t1, t2, t3
    exact_ref[...] = diagonal(trans) / diagonal(t1.astype(f32) + t2.astype(f32))
    sums_ref[...] = jnp.sum(trans, axis=0, keepdims=True)


def gather_kernel(ids_ref, high_ref, mid_ref, low_ref, mine_ref, other_ref):
    groups, frames = ids_ref.shape
    rows = high_ref.shape[0]
    eye = iota((frames, frames), 0) == iota((frames, frames), 1)
    lanes = iota((frames, rows), 1)
    for k in range(groups):
        wide = jnp.where(eye, jnp.broadcast_to(ids_ref[k : k + 1, :], (frames, frames)), 0)
        column = jnp.sum(wide, axis=1, keepdims=True)
        pick = jnp.where(column == lanes, 1.0, 0.0).astype(bf16)
        taken = dot(pick, high_ref[...]) + (dot(pick, mid_ref[...]) + dot(pick, low_ref[...]))
        (other_ref if k % 2 else mine_ref)[k // 2] = taken


def product_kernel(scal_ref, own_ref, recv_ref, trans_ref, trans1_ref, trans2_ref, trans3_ref, exact_ref, sums_ref,
                   init_ref, w_ref, lead_ref, high_ref, low_ref, state_ref, msg_ref, root_ref,
                   scaled_ref, column_ref):
    frames, states = w_ref.shape
    steps = frames // chunks
    first = scal_ref[0]
    w_ref[...] = own_ref[...] + recv_ref[...]
    cat = jnp.concatenate([trans1_ref[...], trans2_ref[...], trans3_ref[...]], axis=0)
    lead_ref[...] = times_col(w_ref[...], cat, states, 3)

    def store(c, y, columns):
        column_ref[c : c + 1, :] = columns
        high_ref[c], low_ref[c] = split2(y)

    def reset(c):
        eye = iota((states, states), 0) == iota((states, states), 1)
        high_ref[c] = jnp.where(eye, 1.0, 0.0).astype(bf16)
        low_ref[c] = jnp.zeros((states, states), bf16)
        column_ref[pl.ds(c, 1), :] = jnp.ones((1, states), f32)

    for c in range(chunks):
        row = w_ref[c * steps : c * steps + 1, :]
        row = row / jnp.sum(sums_ref[...] * row, axis=1, keepdims=True)
        store(c, trans_ref[...] * row, sums_ref[...] * row)
    start_chunk = lax.div(first, steps)
    start_step = lax.rem(first, steps)

    def step(k, carried):
        @pl.when((start_step == k) & (first >= 0) & (first < frames))
        def _():
            reset(start_chunk)

        for c in range(chunks):
            frame = c * steps + k
            total = jnp.sum(lead_ref[pl.ds(frame, 1), :] * column_ref[c : c + 1, :], axis=1, keepdims=True)
            scaled_ref[c : c + 1, :] = w_ref[pl.ds(frame, 1), :] * exact_ref[...] / total
        for c in range(chunks):
            x1, x2 = high_ref[c], low_ref[c]
            y = dot(x1, trans1_ref[...]) + (dot(x1, trans2_ref[...]) + dot(x2, trans1_ref[...]))
            y = y * scaled_ref[c : c + 1, :]
            store(c, y, jnp.sum(y, axis=0, keepdims=True))
        return carried

    lax.fori_loop(1, steps, step, 0)
    for c in range(chunks):

        @pl.when((c + 1) * steps <= first)
        def _():
            reset(c)

    at = chunks
    level = list(range(chunks))
    columns = [column_ref[c : c + 1, :] for c in range(chunks)]
    while len(level) > 1:
        above, found = [], []
        for i in range(0, len(level), 2):
            a1, a2 = high_ref[level[i]], low_ref[level[i]]
            b1, b2 = high_ref[level[i + 1]], low_ref[level[i + 1]]
            column = dot(jnp.broadcast_to(columns[i], (16, states)).astype(bf16), b1)[0:1]
            inverse = 1.0 / jnp.sum(column, axis=1, keepdims=True)
            y = (dot(a1, b1) + (dot(a1, b2) + dot(a2, b1))) * inverse
            high_ref[at], low_ref[at] = split2(y)
            above.append(at)
            found.append(column * inverse)
            at += 1
        level, columns = above, found
    root_ref[...] = y
    init = init_ref[...]
    prior = jnp.broadcast_to(init / jnp.sum(init, axis=1, keepdims=True), (8, states))
    final = jnp.full((8, states), 1.0 / states, f32)
    state_ref[...] = jnp.where(iota((8, states), 0) == 0, prior, final)
    carry_over(prior, final, high_ref, low_ref, msg_ref)


def carry_over(fore, back, high_ref, low_ref, msg_ref):
    states = fore.shape[1]
    root1, root2 = high_ref[2 * chunks - 2], low_ref[2 * chunks - 2]
    ahead = row_times(fore, jnp.concatenate([root1, root2], axis=1), states, 2)
    behind = times_col(back, jnp.concatenate([root1, root2], axis=0), states, 2)
    msg_ref[...] = jnp.where(iota((8, states), 0) == 0, normalize(ahead), normalize(behind))


def merge_state(state, recv, part, parts, turn):
    spot = iota(state.shape, 0)
    take = ((spot == 0) & (part == turn + 1)) | ((spot == 1) & (part == parts - 2 - turn))
    return jnp.where(take, recv, state)


def relay_kernel(parts, turn, scal_ref, state_ref, recv_ref, high_ref, low_ref, out_ref, msg_ref):
    state = merge_state(state_ref[...], recv_ref[...], scal_ref[1], parts, turn - 1)
    out_ref[...] = state
    carry_over(state, state, high_ref, low_ref, msg_ref)


def place(ids_ref, scal_ref, block, turn):
    frames = ids_ref.shape[1]
    square = (frames, frames)
    bits = block.bit_length() - 1
    down, across = iota(square, 0), iota(square, 1)
    row = jnp.broadcast_to(ids_ref[0:1, :], square)
    live = across >= scal_ref[0]
    column = jnp.broadcast_to(jnp.sum(jnp.where(down == across, row, 0), axis=1, keepdims=True), square)
    live_column = down >= scal_ref[0]
    owner_row = jnp.where(live, lax.shift_right_logical(row, bits), -1)
    owner_column = jnp.where(live_column, lax.shift_right_logical(column, bits), -1)
    same = owner_row == owner_column
    rank_row = jnp.sum(jnp.where(same & (down < across), 1, 0), axis=0, keepdims=True)
    rank_column = jnp.sum(jnp.where(same & (across < down), 1, 0), axis=1, keepdims=True)
    most = jnp.max(jnp.where(live[0:1, :], rank_row + 1, 0))
    rank_row = rank_row - rows_sent * turn
    rank_column = rank_column - rows_sent * turn
    fits_row = (rank_row >= 0) & (rank_row < rows_sent) & live[0:1, :]
    fits_column = (rank_column >= 0) & (rank_column < rows_sent) & live_column[:, 0:1]
    local = (column - lax.shift_left(lax.shift_right_logical(column, bits), bits))[:, 0:1]
    return owner_row[0:1, :], rank_row, fits_row, rank_column, fits_column, local, most


def address_kernel(block, scal_ref, turn_ref, ids_ref, pick_ref, meta_ref):
    frames = ids_ref.shape[1]
    lines, states = meta_ref.shape
    turn = turn_ref[0]
    owner, rank, fits, rank_column, fits_column, local, most = place(ids_ref, scal_ref, block, turn)
    spot = jnp.where(fits, owner * slots + rank, -1)
    across = iota((lines, frames), 0)
    totals = (lax.bitwise_and(across, slots - 1) == rows_sent) & (turn == 0)
    pick_ref[...] = jnp.where((across == spot) | totals, 1.0, 0.0).astype(bf16)
    base = scal_ref[2]
    lanes = iota((frames, states), 1)
    ranked = jnp.where(fits_column & (lanes == base + rank_column), (local + 1).astype(f32), 0.0).astype(bf16)
    mine = jnp.where((across == owner * slots + slots - 1) & fits, 1.0, 0.0).astype(bf16)
    last = lax.bitwise_and(iota((lines, 1), 0), slots - 1) == slots - 1
    lanes = iota((1, states), 1)
    meta_ref[...] = jnp.where(last & (lanes == base + rows_sent + 1), most.astype(f32), dot(mine, ranked))


def pack(pick_ref, meta_ref, occupancy, send_ref, base, log_sum):
    high, mid, low = split3(occupancy)
    pick = pick_ref[...]
    lines, states = meta_ref.shape
    last = lax.bitwise_and(iota((lines, 1), 0), slots - 1) == slots - 1
    meta = jnp.where(last & (iota((1, states), 1) == base + rows_sent), log_sum, meta_ref[...])
    send_ref[...] = dot(pick, high) + (dot(pick, mid) + (dot(pick, low) + meta))


def chain_kernel(parts, scal_ref, state_ref, recv_ref, jump_ref, edge_ref, w_ref, lead_ref, high_ref, low_ref, trans1_ref,
                 trans2_ref, exact_ref, sums_ref, pick_ref, meta_ref,
                 keep_ref, away_ref, occ_ref, send_ref, split_ref, leads_ref, fore_ref,
                 back_ref, start_ref, end_ref, post_ref):
    frames, states = w_ref.shape
    steps = frames // chunks
    first = scal_ref[0]
    state = merge_state(state_ref[...], recv_ref[...], scal_ref[1], parts, parts - 3)
    edge1, edge2 = split2(edge_ref[...])
    fore = normalize(row_times(jump_ref[...], jnp.concatenate([edge1, edge2], axis=1), states, 2))
    back = normalize(times_col(jump_ref[...], jnp.concatenate([edge1, edge2], axis=0), states, 2))
    start_ref[0:1, :] = jnp.where(scal_ref[1] == parts - 1, fore[0:1, :], state[0:1, :])
    end_ref[chunks - 1 : chunks, :] = jnp.where(scal_ref[1] == 0, back[1:2, :], state[1:2, :])
    width = chunks
    offsets = {}
    at = 0
    size = chunks
    while size >= 1:
        offsets[chunks // size] = at
        at += size
        size //= 2
    while width > 1:
        half = width // 2
        for g in range(chunks // width):
            left = offsets[half] + 2 * g
            lead = jnp.broadcast_to(start_ref[g * width : g * width + 1, :], (8, states))
            cat = jnp.concatenate([high_ref[left], low_ref[left]], axis=1)
            made = normalize(row_times(lead, cat, states, 2))
            start_ref[g * width + half : g * width + half + 1, :] = made[0:1, :]
            last = g * width + width - 1
            tail = jnp.broadcast_to(end_ref[last : last + 1, :], (8, states))
            cat = jnp.concatenate([high_ref[left + 1], low_ref[left + 1]], axis=0)
            made = normalize(times_col(tail, cat, states, 2))
            end_ref[last - half : last - half + 1, :] = made[0:1, :]
        width = half
    ahead = jnp.concatenate([trans1_ref[...], trans2_ref[...]], axis=1)
    behind = jnp.concatenate([trans1_ref[...], trans2_ref[...]], axis=0)
    exact = exact_ref[...]
    sums = sums_ref[...]
    for h in range(states // 128):
        split_ref[h] = w_ref[:, h * 128 : (h + 1) * 128]
        leads_ref[h] = lead_ref[:, h * 128 : (h + 1) * 128]
    fore = start_ref[...]
    back = end_ref[...]
    logs = jnp.zeros((chunks, 1), f32)
    spots = iota((chunks, 1), 0) * steps
    for k in range(steps):
        scaling = jnp.sum(fore * take(leads_ref, k, steps), axis=1, keepdims=True)
        scaled = take(split_ref, k, steps) * (exact / scaling)
        active = spots + k >= first
        fore = jnp.where(active, row_times(fore, ahead, states, 2) * scaled, fore)
        logs = logs + jnp.where(active, jnp.log(scaling), 0.0)
        put(fore_ref, k, steps, fore)
        j = steps - 1 - k
        put(back_ref, j, steps, back)
        weighed = back * take(split_ref, j, steps)
        inverse = exact / jnp.sum(weighed * sums, axis=1, keepdims=True)
        back = jnp.where(spots + j >= first, times_col(weighed, behind, states, 2) * inverse, back)
    joint = whole(fore_ref) * whole(back_ref)
    occupancy = jnp.where(iota((frames, 1), 0) >= first, normalize(joint), 0.0)
    occ_ref[...] = occupancy
    post_ref[...] = states * occupancy
    side = scal_ref[3]
    half = frames // 2
    keep_ref[...] = post_ref[pl.ds(pl.multiple_of(side * half, half), half), :]
    away_ref[...] = post_ref[pl.ds(pl.multiple_of((1 - side) * half, half), half), :]
    pack(pick_ref, meta_ref, occupancy, send_ref, scal_ref[2], jnp.sum(logs, axis=0, keepdims=True))


def counted(recv_ref, block):
    lines, states = recv_ref.shape
    counts = jnp.zeros((block, states), f32)
    totals = jnp.zeros((1, states), f32)
    slot = lax.bitwise_and(iota((block, states), 1), slots - 1)
    line = lax.bitwise_and(iota((states, states), 0), slots - 1)
    row = (iota((block, states), 0) + 1).astype(f32)
    metas = []
    for g in range(lines // states):
        came = recv_ref[g * states : (g + 1) * states, :]
        meta = jnp.sum(jnp.where(line == slots - 1, came, 0.0), axis=0, keepdims=True)
        totals = totals + jnp.sum(jnp.where(line == rows_sent, came, 0.0), axis=0, keepdims=True)
        pick = jnp.where((meta == row) & (slot < rows_sent), 1.0, 0.0).astype(bf16)
        high, mid, low = split3(came)
        counts = counts + (dot(pick, high) + (dot(pick, mid) + dot(pick, low)))
        metas.append(meta)
    return counts, totals, metas


def emit_update(counts, totals, total_rows):
    return total_rows * (counts + pseudo_count) / (totals + total_rows * pseudo_count)


def final_kernel(block, total_rows, emit_count, length, scal_ref, recv_ref, keep_ref, other_ref,
                 post_ref, new_ref, log_ref, counts_ref, totals_ref, most_ref):
    states = recv_ref.shape[1]
    counts, totals, metas = counted(recv_ref, block)
    counts_ref[...] = counts
    totals_ref[...] = totals
    new_ref[...] = emit_update(counts, totals, total_rows)
    lanes = iota((1, states), 1)
    slot = lax.bitwise_and(lanes, slots - 1)
    most = 0.0
    sums = [0.0, 0.0]
    for g, meta in enumerate(metas):
        most = jnp.maximum(most, jnp.max(jnp.where(slot == rows_sent + 1, meta, 0.0)))
        source = g * (states // slots) + lax.shift_right_logical(lanes, slots.bit_length() - 1)
        column = (lax.bitwise_and(source, emit_count - 1) == scal_ref[4]) & (slot == rows_sent)
        odd = lax.bitwise_and(lax.shift_right_logical(source, emit_count.bit_length() - 1), 1)
        for j in range(2):
            sums[j] = sums[j] + jnp.sum(jnp.where(column & (odd == j), meta, 0.0))
    most_ref[0] = most.astype(jnp.int32)
    for j in range(2):
        log_ref[j] = sums[j] / (length - scal_ref[5 + j]).astype(f32)
    side = scal_ref[3]
    post_ref[side] = keep_ref[...]
    post_ref[1 - side] = other_ref[...]


def pack_kernel(scal_ref, pick_ref, meta_ref, occ_ref, send_ref):
    pack(pick_ref, meta_ref, occ_ref[...], send_ref, scal_ref[2], 0.0)


def more_kernel(block, recv_ref, counts_ref, out_ref):
    counts, _, _ = counted(recv_ref, block)
    out_ref[...] = counts_ref[...] + counts


vmem = pl.BlockSpec(memory_space=pltpu.MemorySpace.VMEM)
smem = pl.BlockSpec(memory_space=pltpu.MemorySpace.SMEM)


def call(kernel, in_specs, out_specs, out_shape, scratch=(), cost=None):
    if cost is not None:
        cost = pl.CostEstimate(flops=cost, bytes_accessed=cost // 100, transcendentals=0)
    return pl.pallas_call(kernel, cost_estimate=cost, in_specs=in_specs, out_specs=out_specs, out_shape=out_shape,
                          scratch_shapes=scratch, compiler_params=pltpu.CompilerParams(vmem_limit_bytes=granted))


def shape(*dims, dtype=f32):
    return jax.ShapeDtypeStruct(dims, dtype)


def update(observed, starts, initial, transition, emission):
    traj_rows, frame_count = observed.shape
    states = transition.shape[0]
    tm_count = lax.axis_size("tm")
    tm_place = lax.axis_index("tm")
    emit_count = lax.axis_size("emit")
    emit_place = lax.axis_index("emit")
    both = ("tm", "emit")
    devices = tm_count * emit_count
    own_rows = emission.shape[0]
    total_rows = own_rows * emit_count
    block = total_rows // devices
    length = frame_count * tm_count
    assert traj_rows == 2 and tm_count % 2 == 0
    frames = 2 * frame_count
    parts = tm_count // 2
    part = tm_place // 2
    side = tm_place % 2
    flat = tm_place * emit_count + emit_place

    kept = jnp.where(side == 0, observed[0:1], observed[1:2])
    given = jnp.where(side == 0, observed[1:2], observed[0:1])
    taken = lax.ppermute(given, "tm", [(i, i ^ 1) for i in range(tm_count)])
    table = shape(own_rows, states, dtype=bf16)
    tables = call(table_kernel, [vmem], [vmem] * 3, [table] * 3, cost=400_000_000)(emission)
    taken, tables = lax.optimization_barrier((taken, tables))
    ids = jnp.where(side == 0, jnp.concatenate([kept, taken], axis=1), jnp.concatenate([taken, kept], axis=1))
    first = jnp.where(side == 0, starts[0], starts[1]) - part * frames
    scal = jnp.stack([first, part, (flat % (states // slots)) * slots, side, emit_place, starts[0], starts[1]])
    scal = scal.astype(jnp.int32)

    def swaps(k):
        return [(i, i ^ k) for i in range(emit_count)]

    near = jnp.concatenate([ids, lax.ppermute(ids, "emit", swaps(1))], axis=0)
    far = [lax.ppermute(near, "emit", swaps(k)) for k in range(2, emit_count, 2)]
    wanted = jnp.concatenate([near] + far, axis=0) - emit_place * own_rows
    half = shape(emit_count // 2, frames, states)
    mine, other = call(gather_kernel, [vmem] * 4, [vmem, vmem], [half, half])(wanted, *tables)
    both_cores = mine + lax.ppermute(other, "emit", swaps(1))
    came = [lax.ppermute(both_cores[k // 2], "emit", swaps(k)) for k in range(2, emit_count, 2)]
    came = sum(came[1:], came[0])
    narrow = shape(states, states, dtype=bf16)
    row = shape(1, states)
    refined = call(matrix_kernel, [vmem], [vmem] * 5, [narrow] * 3 + [row] * 2, cost=400_000_000)(transition)
    came, refined = lax.optimization_barrier((came, refined))
    matrices, exact, sums = refined[:3], refined[3], refined[4]
    nodes = 2 * chunks - 1
    weights, lead, high, low, state, message, root = call(
        product_kernel, [smem] + [vmem] * 9, [vmem] * 7,
        [shape(frames, states), shape(frames, states), shape(nodes, states, states, dtype=bf16),
         shape(nodes, states, states, dtype=bf16), shape(8, states), shape(8, states),
         shape(states, states)],
        [pltpu.VMEM((chunks, states), f32)] * 2,
    )(scal, both_cores[0], came, transition, *matrices, exact, sums, initial.reshape(1, states))

    def address(turn):
        def kernel(*refs):
            address_kernel(block, *refs)

        lines = devices * slots
        return call(kernel, [smem, smem, vmem], [vmem, vmem],
                    [shape(lines, frames, dtype=bf16), shape(lines, states)], cost=400_000_000)(scal, turn, ids)

    pick, meta = address(jnp.zeros((1,), jnp.int32))

    def relay_pairs(turn):
        pairs = []
        for y in range(2):
            pairs.append((2 * turn + y, 2 * turn + 2 + y))
            pairs.append((2 * (parts - 1 - turn) + y, 2 * (parts - 2 - turn) + y))
        return pairs

    def end_pairs(fore, back):
        return [pair for y in range(2) for pair in ((2 * fore + y, 2 * (parts - 1) + y), (2 * back + y, y))]

    assert parts >= 4
    recv = lax.ppermute(message, "tm", relay_pairs(0))
    edge = lax.ppermute(root, "tm", end_pairs(parts - 2, 1))
    for turn in range(1, parts - 2):
        def relay(*refs, turn=turn):
            relay_kernel(parts, turn, *refs)

        state, message = call(
            relay, [smem] + [vmem] * 4, [vmem] * 2, [shape(8, states), shape(8, states)]
        )(scal, state, recv, high, low)
        recv = lax.ppermute(message, "tm", relay_pairs(turn))
    ahead = lax.ppermute(message, "tm", end_pairs(parts - 3, 2))

    def chain(*refs):
        chain_kernel(parts, *refs)

    keep, away, occupancy, send = call(
        chain, [smem] + [vmem] * 14, [vmem] * 4,
        [shape(frame_count, states), shape(frame_count, states), shape(frames, states), shape(devices * slots, states)],
        [pltpu.VMEM((states // 128, frames, 128), f32)] * 4
        + [pltpu.VMEM((chunks, states), f32)] * 2 + [pltpu.VMEM((frames, states), f32)],
    )(scal, state, recv, ahead, edge, weights, lead, high, low, matrices[0], matrices[1], exact, sums, pick, meta)
    other = lax.ppermute(away, "tm", [(i, i ^ 1) for i in range(tm_count)])

    def exchange(sent):
        got = lax.all_to_all(sent.reshape(devices, slots, states), both, 0, 0, tiled=True)
        return got.reshape(devices * slots, states)

    def final(*refs):
        final_kernel(block, total_rows, emit_count, length, *refs)

    posterior, new_emission, loglik, counts, totals, most = call(
        final, [smem, vmem, vmem, vmem], [vmem, vmem, smem, vmem, vmem, smem],
        [shape(2, frame_count, states), shape(block, states), shape(2), shape(block, states), shape(1, states),
         shape(1, dtype=jnp.int32)],
    )(scal, exchange(send), keep, other)

    def another(carried):
        turn, counts, _ = carried

        def more(*refs):
            more_kernel(block, *refs)

        sent = call(pack_kernel, [smem] + [vmem] * 3, vmem, shape(devices * slots, states))(
            scal, *address(turn.reshape(1)), occupancy
        )
        counts = call(more, [vmem, vmem], vmem, shape(block, states))(exchange(sent), counts)
        return turn + 1, counts, emit_update(counts, totals, total_rows)

    _, _, new_emission = lax.while_loop(
        lambda carried: carried[0] * rows_sent < most[0], another, (jnp.int32(1), counts, new_emission)
    )
    return (posterior, new_emission, loglik)


def solution(mesh):
    in_specs = (P("emit", "tm"), P("emit"), P(), P(), P("emit", None))
    out_specs = (P("emit", "tm", None), P(("tm", "emit"), None), P("emit"))
    return jax.shard_map(update, mesh=mesh, in_specs=in_specs, out_specs=out_specs, check_vma=False)
```

```python
import jax
import jax.numpy as jnp
from jax import lax
from jax.experimental import pallas as pl
from jax.experimental.pallas import tpu as pltpu
from jax.sharding import PartitionSpec as P

pseudo_count = 0.01
f32 = jnp.float32
bf16 = jnp.bfloat16
chunks = 8
slots = 16
rows_sent = 14
unrolled = 3
granted = 24 << 20


def split2(x):
    high = x.astype(bf16)
    return high, (x - high.astype(f32)).astype(bf16)


def split3(x):
    high = x.astype(bf16)
    rest = x - high.astype(f32)
    mid = rest.astype(bf16)
    return high, mid, (rest - mid.astype(f32)).astype(bf16)


def iota(shape, dim):
    return lax.broadcasted_iota(jnp.int32, shape, dim)


def dot(a, b):
    return lax.dot_general(a, b, (((1,), (0,)), ((), ())), preferred_element_type=f32)


def dot_nt(a, b):
    return lax.dot_general(a, b, (((1,), (1,)), ((), ())), preferred_element_type=f32)


def stack3(x):
    high = x.astype(bf16).astype(f32)
    rest = x - high
    mid = rest.astype(bf16).astype(f32)
    return jnp.concatenate([high, mid, rest - mid], axis=0).astype(bf16)


def combine(y, rows, states, terms):
    def part(i, j):
        return y[i * rows : (i + 1) * rows, j * states : (j + 1) * states]

    small = part(1, 1) + part(2, 0)
    if terms == 3:
        small = small + part(0, 2)
    return part(0, 0) + ((part(0, 1) + part(1, 0)) + small)


def row_times(x, cat, states, terms):
    return combine(dot(stack3(x), cat), x.shape[0], states, terms)


def times_col(x, cat, states, terms):
    return combine(dot_nt(stack3(x), cat), x.shape[0], states, terms)


def take(ref, start, steps):
    return jnp.concatenate([ref.at[h][pl.ds(start, chunks, stride=steps), :] for h in range(ref.shape[0])], axis=1)


def put(ref, start, steps, x):
    for h in range(ref.shape[0]):
        ref.at[h][pl.ds(start, chunks, stride=steps), :] = x[:, h * 128 : (h + 1) * 128]


def whole(ref):
    return jnp.concatenate([ref[h] for h in range(ref.shape[0])], axis=1)


def normalize(x):
    return x / jnp.sum(x, axis=1, keepdims=True)


def diagonal(x):
    return jnp.sum(jnp.where(iota(x.shape, 0) == iota(x.shape, 1), x, 0.0), axis=0, keepdims=True)


def table_kernel(table_ref, table1_ref, table2_ref, table3_ref):
    table1_ref[...], table2_ref[...], table3_ref[...] = split3(table_ref[...])


def matrix_kernel(trans_ref, trans1_ref, trans2_ref, trans3_ref, exact_ref, sums_ref):
    trans = trans_ref[...]
    t1, t2, t3 = split3(trans)
    trans1_ref[...], trans2_ref[...], trans3_ref[...] = t1, t2, t3
    exact_ref[...] = diagonal(trans) / diagonal(t1.astype(f32) + t2.astype(f32))
    sums_ref[...] = jnp.sum(trans, axis=0, keepdims=True)


def gather_kernel(ids_ref, high_ref, mid_ref, low_ref, mine_ref, other_ref):
    groups, frames = ids_ref.shape
    rows = high_ref.shape[0]
    eye = iota((frames, frames), 0) == iota((frames, frames), 1)
    lanes = iota((frames, rows), 1)
    for k in range(groups):
        wide = jnp.where(eye, jnp.broadcast_to(ids_ref[k : k + 1, :], (frames, frames)), 0)
        column = jnp.sum(wide, axis=1, keepdims=True)
        pick = jnp.where(column == lanes, 1.0, 0.0).astype(bf16)
        taken = dot(pick, high_ref[...]) + (dot(pick, mid_ref[...]) + dot(pick, low_ref[...]))
        (other_ref if k % 2 else mine_ref)[k // 2] = taken


def half_product(half, first, mats, w_ref, lead_ref, high_ref, low_ref, scaled_ref, column_ref, eye_ref):
    trans_ref, trans1_ref, trans2_ref, trans3_ref, exact_ref, sums_ref = mats
    frames, states = w_ref.shape
    count = chunks // 2
    steps = frames // count
    first = first - half * frames
    cat = jnp.concatenate([trans1_ref[...], trans2_ref[...], trans3_ref[...]], axis=0)
    lead_ref[...] = times_col(w_ref[...], cat, states, 3)
    eye = iota((states, states), 0) == iota((states, states), 1)
    eye_ref[...] = jnp.where(eye, 1.0, 0.0).astype(bf16)

    def store(c, k, y, columns):
        live = c * steps + k >= first
        column_ref[c : c + 1, :] = jnp.where(live, columns, 1.0)
        y1, y2 = split2(y)
        high_ref[half * count + c] = jnp.where(live, y1, eye_ref[...])
        low_ref[half * count + c] = jnp.where(live, y2, jnp.zeros_like(y2))

    for c in range(count):
        row = w_ref[c * steps : c * steps + 1, :]
        row = row / jnp.sum(sums_ref[...] * row, axis=1, keepdims=True)
        store(c, 0, trans_ref[...] * row, sums_ref[...] * row)

    def several(i, carried):
        for j in range(unrolled):
            k = 1 + unrolled * i + j
            for c in range(count):
                frame = c * steps + k
                total = jnp.sum(lead_ref[pl.ds(frame, 1), :] * column_ref[c : c + 1, :], axis=1, keepdims=True)
                scaled_ref[c : c + 1, :] = w_ref[pl.ds(frame, 1), :] * exact_ref[...] / total
                x1, x2 = high_ref[half * count + c], low_ref[half * count + c]
                y = dot(x1, trans1_ref[...]) + (dot(x1, trans2_ref[...]) + dot(x2, trans1_ref[...]))
                y = y * scaled_ref[c : c + 1, :]
                store(c, k, y, jnp.sum(y, axis=0, keepdims=True))
        return carried

    assert (steps - 1) % unrolled == 0
    lax.fori_loop(0, (steps - 1) // unrolled, several, 0)
    columns = [column_ref[c : c + 1, :] for c in range(count)]
    level, size, base = half * count, count, chunks
    while size > 1:
        found = []
        for i in range(size // 2):
            to = base + half * (size // 2) + i
            _, column = join(high_ref, low_ref, level + 2 * i, level + 2 * i + 1, to, columns[2 * i])
            found.append(column)
        level = base + half * (size // 2)
        base += size
        size //= 2
        columns = found
    return columns[0]


def join(high_ref, low_ref, left, right, to, column):
    a1, a2 = high_ref[left], low_ref[left]
    b1, b2 = high_ref[right], low_ref[right]
    column = dot(jnp.broadcast_to(column, (16, column.shape[1])).astype(bf16), b1)[0:1]
    inverse = 1.0 / jnp.sum(column, axis=1, keepdims=True)
    y = (dot(a1, b1) + (dot(a1, b2) + dot(a2, b1))) * inverse
    high_ref[to], low_ref[to] = split2(y)
    return y, column * inverse


def split_kernel(scal_ref, own_ref, recv_ref, ids_ref, given_ref):
    half = own_ref.shape[0] // 2
    width = ids_ref.shape[1]
    at = pl.ds(pl.multiple_of((1 - scal_ref[3]) * half, half), half)
    given_ref[0:half, :] = own_ref[at, :] + recv_ref[at, :]
    given_ref[half : half + 8, :] = jnp.zeros((8, own_ref.shape[1]), f32)
    given_ref[half : half + 1, 0:width] = ids_ref[...].astype(f32)


def early_kernel(scal_ref, own_ref, recv_ref, *refs):
    mats, (w_ref, lead_ref, column_out_ref, high_ref, low_ref, scaled_ref, column_ref, eye_ref) = refs[:6], refs[6:]
    half = own_ref.shape[0] // 2
    at = pl.ds(pl.multiple_of(scal_ref[3] * half, half), half)
    w_ref[...] = own_ref[at, :] + recv_ref[at, :]
    column_out_ref[...] = half_product(scal_ref[3], scal_ref[0], mats, w_ref, lead_ref, high_ref, low_ref,
                                       scaled_ref, column_ref, eye_ref)


def late_kernel(scal_ref, taken_ref, early_w_ref, early_lead_ref, early_column_ref, init_ref, *refs):
    mats = refs[:6]
    (w_ref, lead_ref, high_ref, low_ref, state_ref, msg_ref, root_ref, scaled_ref, column_ref, eye_ref,
     half_w_ref, half_lead_ref) = refs[8:]
    half, states = early_w_ref.shape
    side = scal_ref[3]
    half_w_ref[...] = taken_ref[0:half, :]
    column = half_product(1 - side, scal_ref[0], mats, half_w_ref, half_lead_ref, high_ref, low_ref,
                          scaled_ref, column_ref, eye_ref)
    for spot, w, lead in ((side, early_w_ref, early_lead_ref), (1 - side, half_w_ref, half_lead_ref)):
        at = pl.ds(pl.multiple_of(spot * half, half), half)
        w_ref[at, :] = w[...]
        lead_ref[at, :] = lead[...]
    root = 2 * chunks - 2
    column = jnp.where(side == 0, early_column_ref[...], column)
    root_ref[...], _ = join(high_ref, low_ref, root - 2, root - 1, root, column)
    init = init_ref[...]
    prior = jnp.broadcast_to(init / jnp.sum(init, axis=1, keepdims=True), (8, states))
    final = jnp.full((8, states), 1.0 / states, f32)
    state_ref[...] = jnp.where(iota((8, states), 0) == 0, prior, final)
    carry_over(prior, final, high_ref, low_ref, msg_ref)


def carry_over(fore, back, high_ref, low_ref, msg_ref):
    states = fore.shape[1]
    root1, root2 = high_ref[2 * chunks - 2], low_ref[2 * chunks - 2]
    ahead = row_times(fore, jnp.concatenate([root1, root2], axis=1), states, 2)
    behind = times_col(back, jnp.concatenate([root1, root2], axis=0), states, 2)
    msg_ref[...] = jnp.where(iota((8, states), 0) == 0, normalize(ahead), normalize(behind))


def merge_state(state, recv, part, parts, turn):
    spot = iota(state.shape, 0)
    take = ((spot == 0) & (part == turn + 1)) | ((spot == 1) & (part == parts - 2 - turn))
    return jnp.where(take, recv, state)


def relay_kernel(parts, turn, scal_ref, state_ref, recv_ref, high_ref, low_ref, out_ref, msg_ref):
    state = merge_state(state_ref[...], recv_ref[...], scal_ref[1], parts, turn - 1)
    out_ref[...] = state
    carry_over(state, state, high_ref, low_ref, msg_ref)


def place(ids, scal_ref, block, turn):
    frames = ids.shape[1]
    square = (frames, frames)
    bits = block.bit_length() - 1
    down, across = iota(square, 0), iota(square, 1)
    row = jnp.broadcast_to(ids, square)
    live = across >= scal_ref[0]
    column = jnp.broadcast_to(jnp.sum(jnp.where(down == across, row, 0), axis=1, keepdims=True), square)
    live_column = down >= scal_ref[0]
    owner_row = jnp.where(live, lax.shift_right_logical(row, bits), -1)
    owner_column = jnp.where(live_column, lax.shift_right_logical(column, bits), -1)
    same = owner_row == owner_column
    rank_row = jnp.sum(jnp.where(same & (down < across), 1, 0), axis=0, keepdims=True)
    rank_column = jnp.sum(jnp.where(same & (across < down), 1, 0), axis=1, keepdims=True)
    most = jnp.max(jnp.where(live[0:1, :], rank_row + 1, 0))
    rank_row = rank_row - rows_sent * turn
    rank_column = rank_column - rows_sent * turn
    fits_row = (rank_row >= 0) & (rank_row < rows_sent) & live[0:1, :]
    fits_column = (rank_column >= 0) & (rank_column < rows_sent) & live_column[:, 0:1]
    local = (column - lax.shift_left(lax.shift_right_logical(column, bits), bits))[:, 0:1]
    return owner_row[0:1, :], rank_row, fits_row, rank_column, fits_column, local, most


def address_kernel(block, scal_ref, turn_ref, ids_ref, taken_ref, pick_ref, meta_ref):
    frames = ids_ref.shape[1]
    half = frames // 2
    away = taken_ref[half : half + 1, 0:frames].astype(jnp.int32)
    away = jnp.concatenate([away[:, half:], away[:, :half]], axis=1)
    lower = iota((1, frames), 1) < half
    near = (lower & (scal_ref[3] == 0)) | (~lower & (scal_ref[3] == 1))
    ids = jnp.where(near, ids_ref[...], away)
    lines, states = meta_ref.shape
    turn = turn_ref[0]
    owner, rank, fits, rank_column, fits_column, local, most = place(ids, scal_ref, block, turn)
    spot = jnp.where(fits, owner * slots + rank, -1)
    across = iota((lines, frames), 0)
    totals = (lax.bitwise_and(across, slots - 1) == rows_sent) & (turn == 0)
    pick_ref[...] = jnp.where((across == spot) | totals, 1.0, 0.0).astype(bf16)
    base = scal_ref[2]
    lanes = iota((frames, states), 1)
    ranked = jnp.where(fits_column & (lanes == base + rank_column), (local + 1).astype(f32), 0.0).astype(bf16)
    mine = jnp.where((across == owner * slots + slots - 1) & fits, 1.0, 0.0).astype(bf16)
    last = lax.bitwise_and(iota((lines, 1), 0), slots - 1) == slots - 1
    lanes = iota((1, states), 1)
    meta_ref[...] = jnp.where(last & (lanes == base + rows_sent + 1), most.astype(f32), dot(mine, ranked))


def pack(pick_ref, meta_ref, occupancy, send_ref, base, log_sum):
    high, mid, low = split3(occupancy)
    pick = pick_ref[...]
    lines, states = meta_ref.shape
    last = lax.bitwise_and(iota((lines, 1), 0), slots - 1) == slots - 1
    meta = jnp.where(last & (iota((1, states), 1) == base + rows_sent), log_sum, meta_ref[...])
    send_ref[...] = dot(pick, high) + (dot(pick, mid) + (dot(pick, low) + meta))


def chain_kernel(parts, scal_ref, state_ref, recv_ref, jump_ref, edge_ref, w_ref, lead_ref, high_ref, low_ref, trans1_ref,
                 trans2_ref, exact_ref, sums_ref, pick_ref, meta_ref,
                 keep_ref, away_ref, occ_ref, send_ref, split_ref, leads_ref, fore_ref,
                 back_ref, start_ref, end_ref, post_ref):
    frames, states = w_ref.shape
    steps = frames // chunks
    first = scal_ref[0]
    state = merge_state(state_ref[...], recv_ref[...], scal_ref[1], parts, parts - 3)
    edge1, edge2 = split2(edge_ref[...])
    fore = normalize(row_times(jump_ref[...], jnp.concatenate([edge1, edge2], axis=1), states, 2))
    back = normalize(times_col(jump_ref[...], jnp.concatenate([edge1, edge2], axis=0), states, 2))
    start_ref[0:1, :] = jnp.where(scal_ref[1] == parts - 1, fore[0:1, :], state[0:1, :])
    end_ref[chunks - 1 : chunks, :] = jnp.where(scal_ref[1] == 0, back[1:2, :], state[1:2, :])
    width = chunks
    offsets = {}
    at = 0
    size = chunks
    while size >= 1:
        offsets[chunks // size] = at
        at += size
        size //= 2
    while width > 1:
        half = width // 2
        for g in range(chunks // width):
            left = offsets[half] + 2 * g
            lead = jnp.broadcast_to(start_ref[g * width : g * width + 1, :], (8, states))
            cat = jnp.concatenate([high_ref[left], low_ref[left]], axis=1)
            made = normalize(row_times(lead, cat, states, 2))
            start_ref[g * width + half : g * width + half + 1, :] = made[0:1, :]
            last = g * width + width - 1
            tail = jnp.broadcast_to(end_ref[last : last + 1, :], (8, states))
            cat = jnp.concatenate([high_ref[left + 1], low_ref[left + 1]], axis=0)
            made = normalize(times_col(tail, cat, states, 2))
            end_ref[last - half : last - half + 1, :] = made[0:1, :]
        width = half
    ahead = jnp.concatenate([trans1_ref[...], trans2_ref[...]], axis=1)
    behind = jnp.concatenate([trans1_ref[...], trans2_ref[...]], axis=0)
    exact = exact_ref[...]
    sums = sums_ref[...]
    for h in range(states // 128):
        split_ref[h] = w_ref[:, h * 128 : (h + 1) * 128]
        leads_ref[h] = lead_ref[:, h * 128 : (h + 1) * 128]
    fore = start_ref[...]
    back = end_ref[...]
    logs = jnp.zeros((chunks, 1), f32)
    spots = iota((chunks, 1), 0) * steps
    for k in range(steps):
        scaling = jnp.sum(fore * take(leads_ref, k, steps), axis=1, keepdims=True)
        scaled = take(split_ref, k, steps) * (exact / scaling)
        active = spots + k >= first
        fore = jnp.where(active, row_times(fore, ahead, states, 2) * scaled, fore)
        logs = logs + jnp.where(active, jnp.log(scaling), 0.0)
        put(fore_ref, k, steps, fore)
        j = steps - 1 - k
        put(back_ref, j, steps, back)
        weighed = back * take(split_ref, j, steps)
        inverse = exact / jnp.sum(weighed * sums, axis=1, keepdims=True)
        back = jnp.where(spots + j >= first, times_col(weighed, behind, states, 2) * inverse, back)
    joint = whole(fore_ref) * whole(back_ref)
    occupancy = jnp.where(iota((frames, 1), 0) >= first, normalize(joint), 0.0)
    occ_ref[...] = occupancy
    post_ref[...] = states * occupancy
    side = scal_ref[3]
    half = frames // 2
    keep_ref[...] = post_ref[pl.ds(pl.multiple_of(side * half, half), half), :]
    away_ref[...] = post_ref[pl.ds(pl.multiple_of((1 - side) * half, half), half), :]
    pack(pick_ref, meta_ref, occupancy, send_ref, scal_ref[2], jnp.sum(logs, axis=0, keepdims=True))


def counted(recv_ref, block):
    lines, states = recv_ref.shape
    counts = jnp.zeros((block, states), f32)
    totals = jnp.zeros((1, states), f32)
    slot = lax.bitwise_and(iota((block, states), 1), slots - 1)
    line = lax.bitwise_and(iota((states, states), 0), slots - 1)
    row = (iota((block, states), 0) + 1).astype(f32)
    metas = []
    for g in range(lines // states):
        came = recv_ref[g * states : (g + 1) * states, :]
        meta = jnp.sum(jnp.where(line == slots - 1, came, 0.0), axis=0, keepdims=True)
        totals = totals + jnp.sum(jnp.where(line == rows_sent, came, 0.0), axis=0, keepdims=True)
        pick = jnp.where((meta == row) & (slot < rows_sent), 1.0, 0.0).astype(bf16)
        high, mid, low = split3(came)
        counts = counts + (dot(pick, high) + (dot(pick, mid) + dot(pick, low)))
        metas.append(meta)
    return counts, totals, metas


def emit_update(counts, totals, total_rows):
    return total_rows * (counts + pseudo_count) / (totals + total_rows * pseudo_count)


def final_kernel(block, total_rows, emit_count, length, scal_ref, recv_ref, keep_ref, other_ref,
                 post_ref, new_ref, log_ref, counts_ref, totals_ref, most_ref):
    states = recv_ref.shape[1]
    counts, totals, metas = counted(recv_ref, block)
    counts_ref[...] = counts
    totals_ref[...] = totals
    new_ref[...] = emit_update(counts, totals, total_rows)
    lanes = iota((1, states), 1)
    slot = lax.bitwise_and(lanes, slots - 1)
    most = 0.0
    sums = [0.0, 0.0]
    for g, meta in enumerate(metas):
        most = jnp.maximum(most, jnp.max(jnp.where(slot == rows_sent + 1, meta, 0.0)))
        source = g * (states // slots) + lax.shift_right_logical(lanes, slots.bit_length() - 1)
        column = (lax.bitwise_and(source, emit_count - 1) == scal_ref[4]) & (slot == rows_sent)
        odd = lax.bitwise_and(lax.shift_right_logical(source, emit_count.bit_length() - 1), 1)
        for j in range(2):
            sums[j] = sums[j] + jnp.sum(jnp.where(column & (odd == j), meta, 0.0))
    most_ref[0] = most.astype(jnp.int32)
    for j in range(2):
        log_ref[j] = sums[j] / (length - scal_ref[5 + j]).astype(f32)
    side = scal_ref[3]
    post_ref[side] = keep_ref[...]
    post_ref[1 - side] = other_ref[...]


def pack_kernel(scal_ref, pick_ref, meta_ref, occ_ref, send_ref):
    pack(pick_ref, meta_ref, occ_ref[...], send_ref, scal_ref[2], 0.0)


def more_kernel(block, recv_ref, counts_ref, out_ref):
    counts, _, _ = counted(recv_ref, block)
    out_ref[...] = counts_ref[...] + counts


vmem = pl.BlockSpec(memory_space=pltpu.MemorySpace.VMEM)
smem = pl.BlockSpec(memory_space=pltpu.MemorySpace.SMEM)


def call(kernel, in_specs, out_specs, out_shape, scratch=(), cost=None, aliases=None):
    if cost is not None:
        cost = pl.CostEstimate(flops=cost, bytes_accessed=cost // 100, transcendentals=0)
    return pl.pallas_call(kernel, cost_estimate=cost,
                          input_output_aliases=aliases or {}, in_specs=in_specs, out_specs=out_specs, out_shape=out_shape,
                          scratch_shapes=scratch, compiler_params=pltpu.CompilerParams(vmem_limit_bytes=granted))


def shape(*dims, dtype=f32):
    return jax.ShapeDtypeStruct(dims, dtype)


def update(observed, starts, initial, transition, emission):
    traj_rows, frame_count = observed.shape
    states = transition.shape[0]
    tm_count = lax.axis_size("tm")
    tm_place = lax.axis_index("tm")
    emit_count = lax.axis_size("emit")
    emit_place = lax.axis_index("emit")
    both = ("tm", "emit")
    devices = tm_count * emit_count
    own_rows = emission.shape[0]
    total_rows = own_rows * emit_count
    block = total_rows // devices
    length = frame_count * tm_count
    assert traj_rows == 2 and tm_count % 2 == 0
    frames = 2 * frame_count
    parts = tm_count // 2
    part = tm_place // 2
    side = tm_place % 2
    flat = tm_place * emit_count + emit_place

    ids = observed.reshape(1, frames)
    table = shape(own_rows, states, dtype=bf16)
    tables = call(table_kernel, [vmem], [vmem] * 3, [table] * 3, cost=400_000_000)(emission)
    first = jnp.where(side == 0, starts[0], starts[1]) - part * frames
    scal = jnp.stack([first, part, (flat % (states // slots)) * slots, side, emit_place, starts[0], starts[1]])
    scal = scal.astype(jnp.int32)

    def swaps(k):
        return [(i, i ^ k) for i in range(emit_count)]

    near = jnp.concatenate([ids, lax.ppermute(ids, "emit", swaps(1))], axis=0)
    far = [lax.ppermute(near, "emit", swaps(k)) for k in range(2, emit_count, 2)]
    far, tables = lax.optimization_barrier((far, tables))
    wanted = jnp.concatenate([near] + far, axis=0) - emit_place * own_rows
    half = shape(emit_count // 2, frames, states)
    mine, other = call(gather_kernel, [vmem] * 4, [vmem, vmem], [half, half])(wanted, *tables)
    both_cores = mine + lax.ppermute(other, "emit", swaps(1))
    came = [lax.ppermute(both_cores[k // 2], "emit", swaps(k)) for k in range(2, emit_count, 2)]
    came = sum(came[1:], came[0])
    narrow = shape(states, states, dtype=bf16)
    row = shape(1, states)
    refined = call(matrix_kernel, [vmem], [vmem] * 5, [narrow] * 3 + [row] * 2, cost=400_000_000)(transition)
    came, refined = lax.optimization_barrier((came, refined))
    matrices, exact, sums = refined[:3], refined[3], refined[4]
    nodes = 2 * chunks - 1
    given = call(split_kernel, [smem] + [vmem] * 3, vmem, shape(frame_count + 8, states))(
        scal, both_cores[0], came, ids
    )
    taken = lax.ppermute(given, "tm", [(i, i ^ 1) for i in range(tm_count)])
    mats = (transition, *matrices, exact, sums)
    leaves = shape(nodes, states, states, dtype=bf16)
    early_rows = shape(frame_count, states)
    scratch = [pltpu.VMEM((chunks, states), f32)] * 2 + [pltpu.VMEM((states, states), bf16)]
    early_w, early_lead, early_column, high, low = call(
        early_kernel, [smem] + [vmem] * 8, [vmem] * 5, [early_rows, early_rows, row, leaves, leaves],
        scratch, cost=12_000_000_000,
    )(scal, both_cores[0], came, *mats)
    weights, lead, high, low, state, message, root = call(
        late_kernel, [smem] + [vmem] * 13, [vmem] * 7,
        [shape(frames, states), shape(frames, states), leaves, leaves, shape(8, states), shape(8, states),
         shape(states, states)],
        scratch + [pltpu.VMEM((frame_count, states), f32)] * 2, cost=12_000_000_000, aliases={12: 2, 13: 3},
    )(scal, taken, early_w, early_lead, early_column, initial.reshape(1, states), *mats, high, low)

    def address(turn):
        def kernel(*refs):
            address_kernel(block, *refs)

        lines = devices * slots
        return call(kernel, [smem, smem, vmem, vmem], [vmem, vmem],
                    [shape(lines, frames, dtype=bf16), shape(lines, states)], cost=400_000_000)(scal, turn, ids, taken)

    pick, meta = address(jnp.zeros((1,), jnp.int32))

    def relay_pairs(turn):
        pairs = []
        for y in range(2):
            pairs.append((2 * turn + y, 2 * turn + 2 + y))
            pairs.append((2 * (parts - 1 - turn) + y, 2 * (parts - 2 - turn) + y))
        return pairs

    def end_pairs(fore, back):
        return [pair for y in range(2) for pair in ((2 * fore + y, 2 * (parts - 1) + y), (2 * back + y, y))]

    assert parts >= 4
    recv = lax.ppermute(message, "tm", relay_pairs(0))
    edge = lax.ppermute(root, "tm", end_pairs(parts - 2, 1))
    for turn in range(1, parts - 2):
        def relay(*refs, turn=turn):
            relay_kernel(parts, turn, *refs)

        state, message = call(
            relay, [smem] + [vmem] * 4, [vmem] * 2, [shape(8, states), shape(8, states)]
        )(scal, state, recv, high, low)
        recv = lax.ppermute(message, "tm", relay_pairs(turn))
    ahead = lax.ppermute(message, "tm", end_pairs(parts - 3, 2))

    def chain(*refs):
        chain_kernel(parts, *refs)

    keep, away, occupancy, send = call(
        chain, [smem] + [vmem] * 14, [vmem] * 4,
        [shape(frame_count, states), shape(frame_count, states), shape(frames, states), shape(devices * slots, states)],
        [pltpu.VMEM((states // 128, frames, 128), f32)] * 4
        + [pltpu.VMEM((chunks, states), f32)] * 2 + [pltpu.VMEM((frames, states), f32)],
    )(scal, state, recv, ahead, edge, weights, lead, high, low, matrices[0], matrices[1], exact, sums, pick, meta)
    other = lax.ppermute(away, "tm", [(i, i ^ 1) for i in range(tm_count)])

    def exchange(sent):
        got = lax.all_to_all(sent.reshape(devices, slots, states), both, 0, 0, tiled=True)
        return got.reshape(devices * slots, states)

    def final(*refs):
        final_kernel(block, total_rows, emit_count, length, *refs)

    posterior, new_emission, loglik, counts, totals, most = call(
        final, [smem, vmem, vmem, vmem], [vmem, vmem, smem, vmem, vmem, smem],
        [shape(2, frame_count, states), shape(block, states), shape(2), shape(block, states), shape(1, states),
         shape(1, dtype=jnp.int32)],
    )(scal, exchange(send), keep, other)

    def another(carried):
        turn, counts, _ = carried

        def more(*refs):
            more_kernel(block, *refs)

        sent = call(pack_kernel, [smem] + [vmem] * 3, vmem, shape(devices * slots, states))(
            scal, *address(turn.reshape(1)), occupancy
        )
        counts = call(more, [vmem, vmem], vmem, shape(block, states))(exchange(sent), counts)
        return turn + 1, counts, emit_update(counts, totals, total_rows)

    _, _, new_emission = lax.while_loop(
        lambda carried: carried[0] * rows_sent < most[0], another, (jnp.int32(1), counts, new_emission)
    )
    return (posterior, new_emission, loglik)


def solution(mesh):
    in_specs = (P("emit", "tm"), P("emit"), P(), P(), P("emit", None))
    out_specs = (P("emit", "tm", None), P(("tm", "emit"), None), P("emit"))
    return jax.shard_map(update, mesh=mesh, in_specs=in_specs, out_specs=out_specs, check_vma=False)
```

```python
import jax
import jax.numpy as jnp
from jax import lax
from jax.experimental import pallas as pl
from jax.experimental.pallas import tpu as pltpu
from jax.sharding import PartitionSpec as P

pseudo_count = 0.01
f32 = jnp.float32
bf16 = jnp.bfloat16
chunks = 8
slots = 16
rows_sent = 14
unrolled = 3
granted = 24 << 20


def split2(x):
    high = x.astype(bf16)
    return high, (x - high.astype(f32)).astype(bf16)


def split3(x):
    high = x.astype(bf16)
    rest = x - high.astype(f32)
    mid = rest.astype(bf16)
    return high, mid, (rest - mid.astype(f32)).astype(bf16)


def iota(shape, dim):
    return lax.broadcasted_iota(jnp.int32, shape, dim)


def dot(a, b):
    return lax.dot_general(a, b, (((1,), (0,)), ((), ())), preferred_element_type=f32)


def dot_nt(a, b):
    return lax.dot_general(a, b, (((1,), (1,)), ((), ())), preferred_element_type=f32)


def stack3(x):
    high = x.astype(bf16).astype(f32)
    rest = x - high
    mid = rest.astype(bf16).astype(f32)
    return jnp.concatenate([high, mid, rest - mid], axis=0).astype(bf16)


def combine(y, rows, states, terms):
    def part(i, j):
        return y[i * rows : (i + 1) * rows, j * states : (j + 1) * states]

    small = part(1, 1) + part(2, 0)
    if terms == 3:
        small = small + part(0, 2)
    return part(0, 0) + ((part(0, 1) + part(1, 0)) + small)


def row_times(x, cat, states, terms):
    return combine(dot(stack3(x), cat), x.shape[0], states, terms)


def times_col(x, cat, states, terms):
    return combine(dot_nt(stack3(x), cat), x.shape[0], states, terms)


def take(ref, start, steps):
    return jnp.concatenate([ref.at[h][pl.ds(start, chunks, stride=steps), :] for h in range(ref.shape[0])], axis=1)


def put(ref, start, steps, x):
    for h in range(ref.shape[0]):
        ref.at[h][pl.ds(start, chunks, stride=steps), :] = x[:, h * 128 : (h + 1) * 128]


def whole(ref):
    return jnp.concatenate([ref[h] for h in range(ref.shape[0])], axis=1)


def normalize(x):
    return x / jnp.sum(x, axis=1, keepdims=True)


def diagonal(x):
    return jnp.sum(jnp.where(iota(x.shape, 0) == iota(x.shape, 1), x, 0.0), axis=0, keepdims=True)


def table_kernel(table_ref, table1_ref, table2_ref, table3_ref):
    table1_ref[...], table2_ref[...], table3_ref[...] = split3(table_ref[...])


def matrix_kernel(trans_ref, trans1_ref, trans2_ref, trans3_ref, exact_ref, sums_ref):
    trans = trans_ref[...]
    t1, t2, t3 = split3(trans)
    trans1_ref[...], trans2_ref[...], trans3_ref[...] = t1, t2, t3
    exact_ref[...] = diagonal(trans) / diagonal(t1.astype(f32) + t2.astype(f32))
    sums_ref[...] = jnp.sum(trans, axis=0, keepdims=True)


def gather_kernel(ids_ref, high_ref, mid_ref, low_ref, mine_ref, other_ref):
    groups, half = ids_ref.shape[0], ids_ref.shape[1] // 2
    rows, states = high_ref.shape
    side = lax.rem(lax.axis_index("tm"), 2)
    eye = iota((half, half), 0) == iota((half, half), 1)
    lanes = iota((half, rows), 1)
    for k in range(groups):
        one, two = ids_ref[k : k + 1, 0:half], ids_ref[k : k + 1, half : 2 * half]
        picks = []
        for row in (jnp.where(side == 0, one, two), jnp.where(side == 0, two, one)):
            wide = jnp.where(eye, jnp.broadcast_to(row, (half, half)), 0)
            column = jnp.sum(wide, axis=1, keepdims=True)
            picks.append(jnp.where(column == lanes, 1.0, 0.0))
            if k == 0:
                away = row
        pick = jnp.concatenate(picks, axis=0).astype(bf16)
        taken = dot(pick, high_ref[...]) + (dot(pick, mid_ref[...]) + dot(pick, low_ref[...]))
        out_ref = other_ref if k % 2 else mine_ref
        out_ref[k // 2, 0 : 2 * half, :] = taken
        out_ref[k // 2, 2 * half : 2 * half + 8, :] = jnp.zeros((8, states), f32)
        if k == 0:
            out_ref[0, 2 * half : 2 * half + 1, 0:half] = away.astype(f32)


def half_product(half, first, mats, w_ref, lead_ref, high_ref, low_ref, scaled_ref, column_ref, eye_ref):
    trans_ref, trans1_ref, trans2_ref, trans3_ref, exact_ref, sums_ref = mats
    frames, states = w_ref.shape
    count = chunks // 2
    steps = frames // count
    first = first - half * frames
    cat = jnp.concatenate([trans1_ref[...], trans2_ref[...], trans3_ref[...]], axis=0)
    lead_ref[...] = times_col(w_ref[...], cat, states, 3)
    eye = iota((states, states), 0) == iota((states, states), 1)
    eye_ref[...] = jnp.where(eye, 1.0, 0.0).astype(bf16)

    def store(c, k, y, columns):
        live = c * steps + k >= first
        column_ref[c : c + 1, :] = jnp.where(live, columns, 1.0)
        y1, y2 = split2(y)
        high_ref[half * count + c] = jnp.where(live, y1, eye_ref[...])
        low_ref[half * count + c] = jnp.where(live, y2, jnp.zeros_like(y2))

    for c in range(count):
        row = w_ref[c * steps : c * steps + 1, :]
        row = row / jnp.sum(sums_ref[...] * row, axis=1, keepdims=True)
        store(c, 0, trans_ref[...] * row, sums_ref[...] * row)

    def several(i, carried):
        for j in range(unrolled):
            k = 1 + unrolled * i + j
            for c in range(count):
                frame = c * steps + k
                total = jnp.sum(lead_ref[pl.ds(frame, 1), :] * column_ref[c : c + 1, :], axis=1, keepdims=True)
                scaled_ref[c : c + 1, :] = w_ref[pl.ds(frame, 1), :] * exact_ref[...] / total
                x1, x2 = high_ref[half * count + c], low_ref[half * count + c]
                y = dot(x1, trans1_ref[...]) + (dot(x1, trans2_ref[...]) + dot(x2, trans1_ref[...]))
                y = y * scaled_ref[c : c + 1, :]
                store(c, k, y, jnp.sum(y, axis=0, keepdims=True))
        return carried

    assert (steps - 1) % unrolled == 0
    lax.fori_loop(0, (steps - 1) // unrolled, several, 0)
    columns = [column_ref[c : c + 1, :] for c in range(count)]
    level, size, base = half * count, count, chunks
    while size > 1:
        found = []
        for i in range(size // 2):
            to = base + half * (size // 2) + i
            _, column = join(high_ref, low_ref, level + 2 * i, level + 2 * i + 1, to, columns[2 * i])
            found.append(column)
        level = base + half * (size // 2)
        base += size
        size //= 2
        columns = found
    return columns[0]


def join(high_ref, low_ref, left, right, to, column):
    a1, a2 = high_ref[left], low_ref[left]
    b1, b2 = high_ref[right], low_ref[right]
    column = dot(jnp.broadcast_to(column, (16, column.shape[1])).astype(bf16), b1)[0:1]
    inverse = 1.0 / jnp.sum(column, axis=1, keepdims=True)
    y = (dot(a1, b1) + (dot(a1, b2) + dot(a2, b1))) * inverse
    high_ref[to], low_ref[to] = split2(y)
    return y, column * inverse


def early_kernel(count, scal_ref, own_ref, *refs):
    recv_refs, mats = refs[:count], refs[count : count + 6]
    w_ref, lead_ref, column_out_ref, high_ref, low_ref, scaled_ref, column_ref, eye_ref = refs[count + 6 :]
    w = own_ref[0, 0 : w_ref.shape[0], :]
    for r in recv_refs:
        w = w + r[...]
    w_ref[...] = w
    column_out_ref[...] = half_product(scal_ref[3], scal_ref[0], mats, w_ref, lead_ref, high_ref, low_ref,
                                       scaled_ref, column_ref, eye_ref)


def late_kernel(count, scal_ref, taken_ref, early_w_ref, early_lead_ref, early_column_ref, init_ref, *refs):
    more_refs, refs = refs[:count], refs[count:]
    mats = refs[:6]
    (w_ref, lead_ref, high_ref, low_ref, state_ref, msg_ref, root_ref, scaled_ref, column_ref, eye_ref,
     half_w_ref, half_lead_ref) = refs[8:]
    half, states = early_w_ref.shape
    side = scal_ref[3]
    w = taken_ref[0:half, :]
    for r in more_refs:
        w = w + r[...]
    half_w_ref[...] = w
    column = half_product(1 - side, scal_ref[0], mats, half_w_ref, half_lead_ref, high_ref, low_ref,
                          scaled_ref, column_ref, eye_ref)
    for spot, w, lead in ((side, early_w_ref, early_lead_ref), (1 - side, half_w_ref, half_lead_ref)):
        at = pl.ds(pl.multiple_of(spot * half, half), half)
        w_ref[at, :] = w[...]
        lead_ref[at, :] = lead[...]
    root = 2 * chunks - 2
    column = jnp.where(side == 0, early_column_ref[...], column)
    root_ref[...], _ = join(high_ref, low_ref, root - 2, root - 1, root, column)
    init = init_ref[...]
    prior = jnp.broadcast_to(init / jnp.sum(init, axis=1, keepdims=True), (8, states))
    final = jnp.full((8, states), 1.0 / states, f32)
    state_ref[...] = jnp.where(iota((8, states), 0) == 0, prior, final)
    carry_over(prior, final, high_ref, low_ref, msg_ref)


def carry_over(fore, back, high_ref, low_ref, msg_ref):
    states = fore.shape[1]
    root1, root2 = high_ref[2 * chunks - 2], low_ref[2 * chunks - 2]
    ahead = row_times(fore, jnp.concatenate([root1, root2], axis=1), states, 2)
    behind = times_col(back, jnp.concatenate([root1, root2], axis=0), states, 2)
    msg_ref[...] = jnp.where(iota((8, states), 0) == 0, normalize(ahead), normalize(behind))


def merge_state(state, recv, part, parts, turn):
    spot = iota(state.shape, 0)
    take = ((spot == 0) & (part == turn + 1)) | ((spot == 1) & (part == parts - 2 - turn))
    return jnp.where(take, recv, state)


def relay_kernel(parts, turn, scal_ref, state_ref, recv_ref, high_ref, low_ref, out_ref, msg_ref):
    state = merge_state(state_ref[...], recv_ref[...], scal_ref[1], parts, turn - 1)
    out_ref[...] = state
    carry_over(state, state, high_ref, low_ref, msg_ref)


def place(ids, scal_ref, block, turn):
    frames = ids.shape[1]
    square = (frames, frames)
    bits = block.bit_length() - 1
    down, across = iota(square, 0), iota(square, 1)
    row = jnp.broadcast_to(ids, square)
    live = across >= scal_ref[0]
    column = jnp.broadcast_to(jnp.sum(jnp.where(down == across, row, 0), axis=1, keepdims=True), square)
    live_column = down >= scal_ref[0]
    owner_row = jnp.where(live, lax.shift_right_logical(row, bits), -1)
    owner_column = jnp.where(live_column, lax.shift_right_logical(column, bits), -1)
    same = owner_row == owner_column
    rank_row = jnp.sum(jnp.where(same & (down < across), 1, 0), axis=0, keepdims=True)
    rank_column = jnp.sum(jnp.where(same & (across < down), 1, 0), axis=1, keepdims=True)
    most = jnp.max(jnp.where(live[0:1, :], rank_row + 1, 0))
    rank_row = rank_row - rows_sent * turn
    rank_column = rank_column - rows_sent * turn
    fits_row = (rank_row >= 0) & (rank_row < rows_sent) & live[0:1, :]
    fits_column = (rank_column >= 0) & (rank_column < rows_sent) & live_column[:, 0:1]
    local = (column - lax.shift_left(lax.shift_right_logical(column, bits), bits))[:, 0:1]
    return owner_row[0:1, :], rank_row, fits_row, rank_column, fits_column, local, most


def address_kernel(block, own_rows, scal_ref, turn_ref, ids_ref, taken_ref, pick_ref, meta_ref):
    frames = ids_ref.shape[1]
    half = frames // 2
    first = scal_ref[3] == 0
    near = jnp.where(first, ids_ref[:, 0:half], ids_ref[:, half:frames])
    away = taken_ref[half : half + 1, 0:half].astype(jnp.int32) + scal_ref[4] * own_rows
    ids = jnp.concatenate([jnp.where(first, near, away), jnp.where(first, away, near)], axis=1)
    lines, states = meta_ref.shape
    turn = turn_ref[0]
    owner, rank, fits, rank_column, fits_column, local, most = place(ids, scal_ref, block, turn)
    spot = jnp.where(fits, owner * slots + rank, -1)
    across = iota((lines, frames), 0)
    totals = (lax.bitwise_and(across, slots - 1) == rows_sent) & (turn == 0)
    pick_ref[...] = jnp.where((across == spot) | totals, 1.0, 0.0).astype(bf16)
    base = scal_ref[2]
    lanes = iota((frames, states), 1)
    ranked = jnp.where(fits_column & (lanes == base + rank_column), (local + 1).astype(f32), 0.0).astype(bf16)
    mine = jnp.where((across == owner * slots + slots - 1) & fits, 1.0, 0.0).astype(bf16)
    last = lax.bitwise_and(iota((lines, 1), 0), slots - 1) == slots - 1
    lanes = iota((1, states), 1)
    meta_ref[...] = jnp.where(last & (lanes == base + rows_sent + 1), most.astype(f32), dot(mine, ranked))


def pack(pick_ref, meta_ref, occupancy, send_ref, base, log_sum):
    high, mid, low = split3(occupancy)
    pick = pick_ref[...]
    lines, states = meta_ref.shape
    last = lax.bitwise_and(iota((lines, 1), 0), slots - 1) == slots - 1
    meta = jnp.where(last & (iota((1, states), 1) == base + rows_sent), log_sum, meta_ref[...])
    send_ref[...] = dot(pick, high) + (dot(pick, mid) + (dot(pick, low) + meta))


def chain_kernel(parts, scal_ref, state_ref, recv_ref, jump_ref, edge_ref, w_ref, lead_ref, high_ref, low_ref, trans1_ref,
                 trans2_ref, exact_ref, sums_ref, pick_ref, meta_ref,
                 keep_ref, away_ref, occ_ref, send_ref, split_ref, leads_ref, fore_ref,
                 back_ref, start_ref, end_ref, post_ref):
    frames, states = w_ref.shape
    steps = frames // chunks
    first = scal_ref[0]
    state = merge_state(state_ref[...], recv_ref[...], scal_ref[1], parts, parts - 3)
    edge1, edge2 = split2(edge_ref[...])
    fore = normalize(row_times(jump_ref[...], jnp.concatenate([edge1, edge2], axis=1), states, 2))
    back = normalize(times_col(jump_ref[...], jnp.concatenate([edge1, edge2], axis=0), states, 2))
    start_ref[0:1, :] = jnp.where(scal_ref[1] == parts - 1, fore[0:1, :], state[0:1, :])
    end_ref[chunks - 1 : chunks, :] = jnp.where(scal_ref[1] == 0, back[1:2, :], state[1:2, :])
    width = chunks
    offsets = {}
    at = 0
    size = chunks
    while size >= 1:
        offsets[chunks // size] = at
        at += size
        size //= 2
    while width > 1:
        half = width // 2
        for g in range(chunks // width):
            left = offsets[half] + 2 * g
            lead = jnp.broadcast_to(start_ref[g * width : g * width + 1, :], (8, states))
            cat = jnp.concatenate([high_ref[left], low_ref[left]], axis=1)
            made = normalize(row_times(lead, cat, states, 2))
            start_ref[g * width + half : g * width + half + 1, :] = made[0:1, :]
            last = g * width + width - 1
            tail = jnp.broadcast_to(end_ref[last : last + 1, :], (8, states))
            cat = jnp.concatenate([high_ref[left + 1], low_ref[left + 1]], axis=0)
            made = normalize(times_col(tail, cat, states, 2))
            end_ref[last - half : last - half + 1, :] = made[0:1, :]
        width = half
    ahead = jnp.concatenate([trans1_ref[...], trans2_ref[...]], axis=1)
    behind = jnp.concatenate([trans1_ref[...], trans2_ref[...]], axis=0)
    exact = exact_ref[...]
    sums = sums_ref[...]
    for h in range(states // 128):
        split_ref[h] = w_ref[:, h * 128 : (h + 1) * 128]
        leads_ref[h] = lead_ref[:, h * 128 : (h + 1) * 128]
    fore = start_ref[...]
    back = end_ref[...]
    logs = jnp.zeros((chunks, 1), f32)
    spots = iota((chunks, 1), 0) * steps
    for k in range(steps):
        scaling = jnp.sum(fore * take(leads_ref, k, steps), axis=1, keepdims=True)
        scaled = take(split_ref, k, steps) * (exact / scaling)
        active = spots + k >= first
        fore = jnp.where(active, row_times(fore, ahead, states, 2) * scaled, fore)
        logs = logs + jnp.where(active, jnp.log(scaling), 0.0)
        put(fore_ref, k, steps, fore)
        j = steps - 1 - k
        put(back_ref, j, steps, back)
        weighed = back * take(split_ref, j, steps)
        inverse = exact / jnp.sum(weighed * sums, axis=1, keepdims=True)
        back = jnp.where(spots + j >= first, times_col(weighed, behind, states, 2) * inverse, back)
    joint = whole(fore_ref) * whole(back_ref)
    occupancy = jnp.where(iota((frames, 1), 0) >= first, normalize(joint), 0.0)
    occ_ref[...] = occupancy
    post_ref[...] = states * occupancy
    side = scal_ref[3]
    half = frames // 2
    keep_ref[...] = post_ref[pl.ds(pl.multiple_of(side * half, half), half), :]
    away_ref[...] = post_ref[pl.ds(pl.multiple_of((1 - side) * half, half), half), :]
    pack(pick_ref, meta_ref, occupancy, send_ref, scal_ref[2], jnp.sum(logs, axis=0, keepdims=True))


def counted(recv_ref, block):
    lines, states = recv_ref.shape
    counts = jnp.zeros((block, states), f32)
    totals = jnp.zeros((1, states), f32)
    slot = lax.bitwise_and(iota((block, states), 1), slots - 1)
    line = lax.bitwise_and(iota((states, states), 0), slots - 1)
    row = (iota((block, states), 0) + 1).astype(f32)
    metas = []
    for g in range(lines // states):
        came = recv_ref[g * states : (g + 1) * states, :]
        meta = jnp.sum(jnp.where(line == slots - 1, came, 0.0), axis=0, keepdims=True)
        totals = totals + jnp.sum(jnp.where(line == rows_sent, came, 0.0), axis=0, keepdims=True)
        pick = jnp.where((meta == row) & (slot < rows_sent), 1.0, 0.0).astype(bf16)
        high, mid, low = split3(came)
        counts = counts + (dot(pick, high) + (dot(pick, mid) + dot(pick, low)))
        metas.append(meta)
    return counts, totals, metas


def emit_update(counts, totals, total_rows):
    return total_rows * (counts + pseudo_count) / (totals + total_rows * pseudo_count)


def final_kernel(block, total_rows, emit_count, length, scal_ref, recv_ref, new_ref, log_ref,
                 counts_ref, totals_ref, most_ref):
    states = recv_ref.shape[1]
    counts, totals, metas = counted(recv_ref, block)
    counts_ref[...] = counts
    totals_ref[...] = totals
    new_ref[...] = emit_update(counts, totals, total_rows)
    lanes = iota((1, states), 1)
    slot = lax.bitwise_and(lanes, slots - 1)
    most = 0.0
    sums = [0.0, 0.0]
    for g, meta in enumerate(metas):
        most = jnp.maximum(most, jnp.max(jnp.where(slot == rows_sent + 1, meta, 0.0)))
        source = g * (states // slots) + lax.shift_right_logical(lanes, slots.bit_length() - 1)
        column = (lax.bitwise_and(source, emit_count - 1) == scal_ref[4]) & (slot == rows_sent)
        odd = lax.bitwise_and(lax.shift_right_logical(source, emit_count.bit_length() - 1), 1)
        for j in range(2):
            sums[j] = sums[j] + jnp.sum(jnp.where(column & (odd == j), meta, 0.0))
    most_ref[0] = most.astype(jnp.int32)
    for j in range(2):
        log_ref[j] = sums[j] / (length - scal_ref[5 + j]).astype(f32)


def posterior_kernel(scal_ref, keep_ref, other_ref, post_ref):
    side = scal_ref[3]
    post_ref[side] = keep_ref[...]
    post_ref[1 - side] = other_ref[...]


def pack_kernel(scal_ref, pick_ref, meta_ref, occ_ref, send_ref):
    pack(pick_ref, meta_ref, occ_ref[...], send_ref, scal_ref[2], 0.0)


def more_kernel(block, recv_ref, counts_ref, out_ref):
    counts, _, _ = counted(recv_ref, block)
    out_ref[...] = counts_ref[...] + counts


vmem = pl.BlockSpec(memory_space=pltpu.MemorySpace.VMEM)
smem = pl.BlockSpec(memory_space=pltpu.MemorySpace.SMEM)


def call(kernel, in_specs, out_specs, out_shape, scratch=(), cost=None, aliases=None):
    if cost is not None:
        cost = pl.CostEstimate(flops=cost, bytes_accessed=cost // 100, transcendentals=0)
    return pl.pallas_call(kernel, cost_estimate=cost,
                          input_output_aliases=aliases or {}, in_specs=in_specs, out_specs=out_specs, out_shape=out_shape,
                          scratch_shapes=scratch, compiler_params=pltpu.CompilerParams(vmem_limit_bytes=granted))


def shape(*dims, dtype=f32):
    return jax.ShapeDtypeStruct(dims, dtype)


def update(observed, starts, initial, transition, emission):
    traj_rows, frame_count = observed.shape
    states = transition.shape[0]
    tm_count = lax.axis_size("tm")
    tm_place = lax.axis_index("tm")
    emit_count = lax.axis_size("emit")
    emit_place = lax.axis_index("emit")
    both = ("tm", "emit")
    devices = tm_count * emit_count
    own_rows = emission.shape[0]
    total_rows = own_rows * emit_count
    block = total_rows // devices
    length = frame_count * tm_count
    assert traj_rows == 2 and tm_count % 2 == 0
    frames = 2 * frame_count
    parts = tm_count // 2
    part = tm_place // 2
    side = tm_place % 2
    flat = tm_place * emit_count + emit_place

    ids = observed.reshape(1, frames)
    table = shape(own_rows, states, dtype=bf16)
    tables = call(table_kernel, [vmem], [vmem] * 3, [table] * 3, cost=400_000_000)(emission)
    first = jnp.where(side == 0, starts[0], starts[1]) - part * frames
    scal = jnp.stack([first, part, (flat % (states // slots)) * slots, side, emit_place, starts[0], starts[1]])
    scal = scal.astype(jnp.int32)

    def swaps(k):
        return [(i, i ^ k) for i in range(emit_count)]

    near = jnp.concatenate([ids, lax.ppermute(ids, "emit", swaps(1))], axis=0)
    far = [lax.ppermute(near, "emit", swaps(k)) for k in range(2, emit_count, 2)]
    far, tables = lax.optimization_barrier((far, tables))
    wanted = jnp.concatenate([near] + far, axis=0) - emit_place * own_rows
    gathered = shape(emit_count // 2, frames + 8, states)
    mine, other = call(gather_kernel, [vmem] * 4, [vmem, vmem], [gathered] * 2)(wanted, *tables)
    summed = mine + lax.ppermute(other, "emit", swaps(1))
    came, more = [], []
    for k in range(2, emit_count, 2):
        came.append(lax.ppermute(summed[k // 2, 0:frame_count], "emit", swaps(k)))
    taken = lax.ppermute(summed[0, frame_count:], "tm", [(i, i ^ 1) for i in range(tm_count)])
    for k in range(2, emit_count, 2):
        pairs = [(i, (i // emit_count ^ 1) * emit_count + (i % emit_count ^ k)) for i in range(devices)]
        more.append(lax.ppermute(summed[k // 2, frame_count:frames], both, pairs))
    narrow = shape(states, states, dtype=bf16)
    row = shape(1, states)
    refined = call(matrix_kernel, [vmem], [vmem] * 5, [narrow] * 3 + [row] * 2, cost=400_000_000)(transition)
    came, refined = lax.optimization_barrier((came, refined))
    matrices, exact, sums = refined[:3], refined[3], refined[4]
    nodes = 2 * chunks - 1
    count = len(came)

    def early(*refs):
        early_kernel(count, *refs)

    def late(*refs):
        late_kernel(count, *refs)

    mats = (transition, *matrices, exact, sums)
    leaves = shape(nodes, states, states, dtype=bf16)
    early_rows = shape(frame_count, states)
    scratch = [pltpu.VMEM((chunks, states), f32)] * 2 + [pltpu.VMEM((states, states), bf16)]
    early_w, early_lead, early_column, high, low = call(
        early, [smem] + [vmem] * (7 + count), [vmem] * 5, [early_rows, early_rows, row, leaves, leaves],
        scratch, cost=12_000_000_000,
    )(scal, summed, *came, *mats)
    weights, lead, high, low, state, message, root = call(
        late, [smem] + [vmem] * (13 + count), [vmem] * 7,
        [shape(frames, states), shape(frames, states), leaves, leaves, shape(8, states), shape(8, states),
         shape(states, states)],
        scratch + [pltpu.VMEM((frame_count, states), f32)] * 2, cost=12_000_000_000, aliases={12 + count: 2, 13 + count: 3},
    )(scal, taken, early_w, early_lead, early_column, initial.reshape(1, states), *more, *mats, high, low)

    def address(turn):
        def kernel(*refs):
            address_kernel(block, own_rows, *refs)

        lines = devices * slots
        return call(kernel, [smem, smem, vmem, vmem], [vmem, vmem],
                    [shape(lines, frames, dtype=bf16), shape(lines, states)], cost=400_000_000)(scal, turn, ids, taken)

    pick, meta = address(jnp.zeros((1,), jnp.int32))

    def relay_pairs(turn):
        pairs = []
        for y in range(2):
            pairs.append((2 * turn + y, 2 * turn + 2 + y))
            pairs.append((2 * (parts - 1 - turn) + y, 2 * (parts - 2 - turn) + y))
        return pairs

    def end_pairs(fore, back):
        return [pair for y in range(2) for pair in ((2 * fore + y, 2 * (parts - 1) + y), (2 * back + y, y))]

    assert parts >= 4
    recv = lax.ppermute(message, "tm", relay_pairs(0))
    edge = lax.ppermute(root, "tm", end_pairs(parts - 2, 1))
    for turn in range(1, parts - 2):
        def relay(*refs, turn=turn):
            relay_kernel(parts, turn, *refs)

        state, message = call(
            relay, [smem] + [vmem] * 4, [vmem] * 2, [shape(8, states), shape(8, states)]
        )(scal, state, recv, high, low)
        recv = lax.ppermute(message, "tm", relay_pairs(turn))
    ahead = lax.ppermute(message, "tm", end_pairs(parts - 3, 2))

    def chain(*refs):
        chain_kernel(parts, *refs)

    keep, away, occupancy, send = call(
        chain, [smem] + [vmem] * 14, [vmem] * 4,
        [shape(frame_count, states), shape(frame_count, states), shape(frames, states), shape(devices * slots, states)],
        [pltpu.VMEM((states // 128, frames, 128), f32)] * 4
        + [pltpu.VMEM((chunks, states), f32)] * 2 + [pltpu.VMEM((frames, states), f32)],
    )(scal, state, recv, ahead, edge, weights, lead, high, low, matrices[0], matrices[1], exact, sums, pick, meta)
    other = lax.ppermute(away, "tm", [(i, i ^ 1) for i in range(tm_count)])

    def exchange(sent):
        got = lax.all_to_all(sent.reshape(devices, slots, states), both, 0, 0, tiled=True)
        return got.reshape(devices * slots, states)

    def final(*refs):
        final_kernel(block, total_rows, emit_count, length, *refs)

    sent = exchange(send)
    posterior = call(posterior_kernel, [smem, vmem, vmem], vmem, shape(2, frame_count, states),
                     cost=100_000_000)(scal, keep, other)
    new_emission, loglik, counts, totals, most = call(
        final, [smem, vmem], [vmem, smem, vmem, vmem, smem],
        [shape(block, states), shape(2), shape(block, states), shape(1, states), shape(1, dtype=jnp.int32)],
    )(scal, sent)

    def another(carried):
        turn, counts, _ = carried

        def more(*refs):
            more_kernel(block, *refs)

        sent = call(pack_kernel, [smem] + [vmem] * 3, vmem, shape(devices * slots, states))(
            scal, *address(turn.reshape(1)), occupancy
        )
        counts = call(more, [vmem, vmem], vmem, shape(block, states))(exchange(sent), counts)
        return turn + 1, counts, emit_update(counts, totals, total_rows)

    _, _, new_emission = lax.while_loop(
        lambda carried: carried[0] * rows_sent < most[0], another, (jnp.int32(1), counts, new_emission)
    )
    return (posterior, new_emission, loglik)


def solution(mesh):
    in_specs = (P("emit", "tm"), P("emit"), P(), P(), P("emit", None))
    out_specs = (P("emit", "tm", None), P(("tm", "emit"), None), P("emit"))
    return jax.shard_map(update, mesh=mesh, in_specs=in_specs, out_specs=out_specs, check_vma=False)
```

```python
import jax
import jax.numpy as jnp
from jax import lax
from jax.experimental import pallas as pl
from jax.experimental.pallas import tpu as pltpu
from jax.sharding import PartitionSpec as P

pseudo_count = 0.01
f32 = jnp.float32
bf16 = jnp.bfloat16
chunks = 8
slots = 16
rows_sent = 14
unrolled = 5
granted = 24 << 20


def split2(x):
    high = x.astype(bf16)
    return high, (x - high.astype(f32)).astype(bf16)


def split3(x):
    high = x.astype(bf16)
    rest = x - high.astype(f32)
    mid = rest.astype(bf16)
    return high, mid, (rest - mid.astype(f32)).astype(bf16)


def iota(shape, dim):
    return lax.broadcasted_iota(jnp.int32, shape, dim)


def dot(a, b):
    return lax.dot_general(a, b, (((1,), (0,)), ((), ())), preferred_element_type=f32)


def dot_nt(a, b):
    return lax.dot_general(a, b, (((1,), (1,)), ((), ())), preferred_element_type=f32)


def stack3(x):
    high = x.astype(bf16).astype(f32)
    rest = x - high
    mid = rest.astype(bf16).astype(f32)
    return jnp.concatenate([high, mid, rest - mid], axis=0).astype(bf16)


def combine(y, rows, states, terms):
    def part(i, j):
        return y[i * rows : (i + 1) * rows, j * states : (j + 1) * states]

    small = part(1, 1) + part(2, 0)
    if terms == 3:
        small = small + part(0, 2)
    return part(0, 0) + ((part(0, 1) + part(1, 0)) + small)


def row_times(x, cat, states, terms):
    return combine(dot(stack3(x), cat), x.shape[0], states, terms)


def times_col(x, cat, states, terms):
    return combine(dot_nt(stack3(x), cat), x.shape[0], states, terms)


def take(ref, start, steps):
    return jnp.concatenate([ref.at[h][pl.ds(start, chunks, stride=steps), :] for h in range(ref.shape[0])], axis=1)


def put(ref, start, steps, x):
    for h in range(ref.shape[0]):
        ref.at[h][pl.ds(start, chunks, stride=steps), :] = x[:, h * 128 : (h + 1) * 128]


def whole(ref):
    return jnp.concatenate([ref[h] for h in range(ref.shape[0])], axis=1)


def normalize(x):
    return x / jnp.sum(x, axis=1, keepdims=True)


def diagonal(x):
    return jnp.sum(jnp.where(iota(x.shape, 0) == iota(x.shape, 1), x, 0.0), axis=0, keepdims=True)


def table_kernel(table_ref, table1_ref, table2_ref, table3_ref):
    table1_ref[...], table2_ref[...], table3_ref[...] = split3(table_ref[...])


def matrix_kernel(trans_ref, trans1_ref, trans2_ref, trans3_ref, exact_ref, sums_ref):
    trans = trans_ref[...]
    t1, t2, t3 = split3(trans)
    trans1_ref[...], trans2_ref[...], trans3_ref[...] = t1, t2, t3
    exact_ref[...] = diagonal(trans) / diagonal(t1.astype(f32) + t2.astype(f32))
    sums_ref[...] = jnp.sum(trans, axis=0, keepdims=True)


def gather_kernel(ids_ref, high_ref, mid_ref, low_ref, mine_ref, other_ref):
    groups, half = ids_ref.shape[0], ids_ref.shape[1] // 2
    rows, states = high_ref.shape
    side = lax.rem(lax.axis_index("tm"), 2)
    eye = iota((half, half), 0) == iota((half, half), 1)
    lanes = iota((half, rows), 1)
    for k in range(groups):
        one, two = ids_ref[k : k + 1, 0:half], ids_ref[k : k + 1, half : 2 * half]
        picks = []
        for row in (jnp.where(side == 0, one, two), jnp.where(side == 0, two, one)):
            wide = jnp.where(eye, jnp.broadcast_to(row, (half, half)), 0)
            column = jnp.sum(wide, axis=1, keepdims=True)
            picks.append(jnp.where(column == lanes, 1.0, 0.0))
            if k == 0:
                away = row
        pick = jnp.concatenate(picks, axis=0).astype(bf16)
        taken = dot(pick, high_ref[...]) + (dot(pick, mid_ref[...]) + dot(pick, low_ref[...]))
        out_ref = other_ref if k % 2 else mine_ref
        out_ref[k // 2, 0 : 2 * half, :] = taken
        out_ref[k // 2, 2 * half : 2 * half + 8, :] = jnp.zeros((8, states), f32)
        if k == 0:
            out_ref[0, 2 * half : 2 * half + 1, 0:half] = away.astype(f32)


def half_product(half, first, mats, w_ref, lead_ref, high_ref, low_ref, scaled_ref, column_ref, eye_ref):
    trans_ref, trans1_ref, trans2_ref, trans3_ref, exact_ref, sums_ref = mats
    frames, states = w_ref.shape
    count = chunks // 2
    steps = frames // count
    first = first - half * frames
    cat = jnp.concatenate([trans1_ref[...], trans2_ref[...], trans3_ref[...]], axis=0)
    lead_ref[...] = times_col(w_ref[...], cat, states, 3)
    eye = iota((states, states), 0) == iota((states, states), 1)
    eye_ref[...] = jnp.where(eye, 1.0, 0.0).astype(bf16)

    def store(c, k, y, columns):
        live = c * steps + k >= first
        column_ref[c : c + 1, :] = jnp.where(live, columns, 1.0)
        y1, y2 = split2(y)
        high_ref[half * count + c] = jnp.where(live, y1, eye_ref[...])
        low_ref[half * count + c] = jnp.where(live, y2, jnp.zeros_like(y2))

    for c in range(count):
        row = w_ref[c * steps : c * steps + 1, :]
        row = row / jnp.sum(sums_ref[...] * row, axis=1, keepdims=True)
        store(c, 0, trans_ref[...] * row, sums_ref[...] * row)

    def several(i, carried):
        for j in range(unrolled):
            k = 1 + unrolled * i + j
            for c in range(count):
                frame = c * steps + k
                total = jnp.sum(lead_ref[pl.ds(frame, 1), :] * column_ref[c : c + 1, :], axis=1, keepdims=True)
                scaled_ref[c : c + 1, :] = w_ref[pl.ds(frame, 1), :] * exact_ref[...] / total
                x1, x2 = high_ref[half * count + c], low_ref[half * count + c]
                y = dot(x1, trans1_ref[...]) + (dot(x1, trans2_ref[...]) + dot(x2, trans1_ref[...]))
                y = y * scaled_ref[c : c + 1, :]
                store(c, k, y, jnp.sum(y, axis=0, keepdims=True))
        return carried

    assert (steps - 1) % unrolled == 0
    lax.fori_loop(0, (steps - 1) // unrolled, several, 0)
    columns = [column_ref[c : c + 1, :] for c in range(count)]
    level, size, base = half * count, count, chunks
    while size > 1:
        found = []
        for i in range(size // 2):
            to = base + half * (size // 2) + i
            _, column = join(high_ref, low_ref, level + 2 * i, level + 2 * i + 1, to, columns[2 * i])
            found.append(column)
        level = base + half * (size // 2)
        base += size
        size //= 2
        columns = found
    return columns[0]


def join(high_ref, low_ref, left, right, to, column):
    a1, a2 = high_ref[left], low_ref[left]
    b1, b2 = high_ref[right], low_ref[right]
    column = dot(jnp.broadcast_to(column, (16, column.shape[1])).astype(bf16), b1)[0:1]
    inverse = 1.0 / jnp.sum(column, axis=1, keepdims=True)
    y = (dot(a1, b1) + (dot(a1, b2) + dot(a2, b1))) * inverse
    high_ref[to], low_ref[to] = split2(y)
    return y, column * inverse


def early_kernel(count, scal_ref, own_ref, *refs):
    recv_refs, mats = refs[:count], refs[count : count + 6]
    w_ref, lead_ref, column_out_ref, high_ref, low_ref, scaled_ref, column_ref, eye_ref = refs[count + 6 :]
    w = own_ref[0, 0 : w_ref.shape[0], :]
    for r in recv_refs:
        w = w + r[...]
    w_ref[...] = w
    column_out_ref[...] = half_product(scal_ref[3], scal_ref[0], mats, w_ref, lead_ref, high_ref, low_ref,
                                       scaled_ref, column_ref, eye_ref)


def late_kernel(count, scal_ref, taken_ref, early_w_ref, early_lead_ref, early_column_ref, init_ref, *refs):
    more_refs, refs = refs[:count], refs[count:]
    mats = refs[:6]
    (w_ref, lead_ref, high_ref, low_ref, state_ref, msg_ref, root_ref, scaled_ref, column_ref, eye_ref,
     half_w_ref, half_lead_ref) = refs[8:]
    half, states = early_w_ref.shape
    side = scal_ref[3]
    w = taken_ref[0:half, :]
    for r in more_refs:
        w = w + r[...]
    half_w_ref[...] = w
    column = half_product(1 - side, scal_ref[0], mats, half_w_ref, half_lead_ref, high_ref, low_ref,
                          scaled_ref, column_ref, eye_ref)
    for spot, w, lead in ((side, early_w_ref, early_lead_ref), (1 - side, half_w_ref, half_lead_ref)):
        at = pl.ds(pl.multiple_of(spot * half, half), half)
        w_ref[at, :] = w[...]
        lead_ref[at, :] = lead[...]
    root = 2 * chunks - 2
    column = jnp.where(side == 0, early_column_ref[...], column)
    root_ref[...], _ = join(high_ref, low_ref, root - 2, root - 1, root, column)
    init = init_ref[...]
    prior = jnp.broadcast_to(init / jnp.sum(init, axis=1, keepdims=True), (8, states))
    final = jnp.full((8, states), 1.0 / states, f32)
    state_ref[...] = jnp.where(iota((8, states), 0) == 0, prior, final)
    carry_over(prior, final, high_ref, low_ref, msg_ref)


def carry_over(fore, back, high_ref, low_ref, msg_ref):
    states = fore.shape[1]
    root1, root2 = high_ref[2 * chunks - 2], low_ref[2 * chunks - 2]
    ahead = row_times(fore, jnp.concatenate([root1, root2], axis=1), states, 2)
    behind = times_col(back, jnp.concatenate([root1, root2], axis=0), states, 2)
    msg_ref[...] = jnp.where(iota((8, states), 0) == 0, normalize(ahead), normalize(behind))


def merge_state(state, recv, part, parts, turn):
    spot = iota(state.shape, 0)
    take = ((spot == 0) & (part == turn + 1)) | ((spot == 1) & (part == parts - 2 - turn))
    return jnp.where(take, recv, state)


def relay_kernel(parts, turn, scal_ref, state_ref, recv_ref, high_ref, low_ref, out_ref, msg_ref):
    state = merge_state(state_ref[...], recv_ref[...], scal_ref[1], parts, turn - 1)
    out_ref[...] = state
    carry_over(state, state, high_ref, low_ref, msg_ref)


def place(ids, scal_ref, block, turn):
    frames = ids.shape[1]
    square = (frames, frames)
    bits = block.bit_length() - 1
    down, across = iota(square, 0), iota(square, 1)
    row = jnp.broadcast_to(ids, square)
    live = across >= scal_ref[0]
    column = jnp.broadcast_to(jnp.sum(jnp.where(down == across, row, 0), axis=1, keepdims=True), square)
    live_column = down >= scal_ref[0]
    owner_row = jnp.where(live, lax.shift_right_logical(row, bits), -1)
    owner_column = jnp.where(live_column, lax.shift_right_logical(column, bits), -1)
    same = owner_row == owner_column
    rank_row = jnp.sum(jnp.where(same & (down < across), 1, 0), axis=0, keepdims=True)
    rank_column = jnp.sum(jnp.where(same & (across < down), 1, 0), axis=1, keepdims=True)
    most = jnp.max(jnp.where(live[0:1, :], rank_row + 1, 0))
    rank_row = rank_row - rows_sent * turn
    rank_column = rank_column - rows_sent * turn
    fits_row = (rank_row >= 0) & (rank_row < rows_sent) & live[0:1, :]
    fits_column = (rank_column >= 0) & (rank_column < rows_sent) & live_column[:, 0:1]
    local = (column - lax.shift_left(lax.shift_right_logical(column, bits), bits))[:, 0:1]
    return owner_row[0:1, :], rank_row, fits_row, rank_column, fits_column, local, most


def address_kernel(block, own_rows, scal_ref, turn_ref, ids_ref, taken_ref, pick_ref, meta_ref):
    frames = ids_ref.shape[1]
    half = frames // 2
    first = scal_ref[3] == 0
    near = jnp.where(first, ids_ref[:, 0:half], ids_ref[:, half:frames])
    away = taken_ref[half : half + 1, 0:half].astype(jnp.int32) + scal_ref[4] * own_rows
    ids = jnp.concatenate([jnp.where(first, near, away), jnp.where(first, away, near)], axis=1)
    lines, states = meta_ref.shape
    turn = turn_ref[0]
    owner, rank, fits, rank_column, fits_column, local, most = place(ids, scal_ref, block, turn)
    spot = jnp.where(fits, owner * slots + rank, -1)
    across = iota((lines, frames), 0)
    totals = (lax.bitwise_and(across, slots - 1) == rows_sent) & (turn == 0)
    pick_ref[...] = jnp.where((across == spot) | totals, 1.0, 0.0).astype(bf16)
    base = scal_ref[2]
    lanes = iota((frames, states), 1)
    ranked = jnp.where(fits_column & (lanes == base + rank_column), (local + 1).astype(f32), 0.0).astype(bf16)
    mine = jnp.where((across == owner * slots + slots - 1) & fits, 1.0, 0.0).astype(bf16)
    last = lax.bitwise_and(iota((lines, 1), 0), slots - 1) == slots - 1
    lanes = iota((1, states), 1)
    meta_ref[...] = jnp.where(last & (lanes == base + rows_sent + 1), most.astype(f32), dot(mine, ranked))


def pack(pick_ref, meta_ref, occupancy, send_ref, base, log_sum):
    high, mid, low = split3(occupancy)
    pick = pick_ref[...]
    lines, states = meta_ref.shape
    last = lax.bitwise_and(iota((lines, 1), 0), slots - 1) == slots - 1
    meta = jnp.where(last & (iota((1, states), 1) == base + rows_sent), log_sum, meta_ref[...])
    send_ref[...] = dot(pick, high) + (dot(pick, mid) + (dot(pick, low) + meta))


def chain_kernel(parts, scal_ref, state_ref, recv_ref, jump_ref, edge_ref, w_ref, lead_ref, high_ref, low_ref, trans1_ref,
                 trans2_ref, exact_ref, sums_ref, pick_ref, meta_ref,
                 keep_ref, away_ref, occ_ref, send_ref, split_ref, leads_ref, fore_ref,
                 back_ref, start_ref, end_ref, post_ref):
    frames, states = w_ref.shape
    steps = frames // chunks
    first = scal_ref[0]
    state = merge_state(state_ref[...], recv_ref[...], scal_ref[1], parts, parts - 3)
    edge1, edge2 = split2(edge_ref[...])
    fore = normalize(row_times(jump_ref[...], jnp.concatenate([edge1, edge2], axis=1), states, 2))
    back = normalize(times_col(jump_ref[...], jnp.concatenate([edge1, edge2], axis=0), states, 2))
    start_ref[0:1, :] = jnp.where(scal_ref[1] == parts - 1, fore[0:1, :], state[0:1, :])
    end_ref[chunks - 1 : chunks, :] = jnp.where(scal_ref[1] == 0, back[1:2, :], state[1:2, :])
    width = chunks
    offsets = {}
    at = 0
    size = chunks
    while size >= 1:
        offsets[chunks // size] = at
        at += size
        size //= 2
    while width > 1:
        half = width // 2
        for g in range(chunks // width):
            left = offsets[half] + 2 * g
            lead = jnp.broadcast_to(start_ref[g * width : g * width + 1, :], (8, states))
            cat = jnp.concatenate([high_ref[left], low_ref[left]], axis=1)
            made = normalize(row_times(lead, cat, states, 2))
            start_ref[g * width + half : g * width + half + 1, :] = made[0:1, :]
            last = g * width + width - 1
            tail = jnp.broadcast_to(end_ref[last : last + 1, :], (8, states))
            cat = jnp.concatenate([high_ref[left + 1], low_ref[left + 1]], axis=0)
            made = normalize(times_col(tail, cat, states, 2))
            end_ref[last - half : last - half + 1, :] = made[0:1, :]
        width = half
    ahead = jnp.concatenate([trans1_ref[...], trans2_ref[...]], axis=1)
    behind = jnp.concatenate([trans1_ref[...], trans2_ref[...]], axis=0)
    exact = exact_ref[...]
    sums = sums_ref[...]
    for h in range(states // 128):
        split_ref[h] = w_ref[:, h * 128 : (h + 1) * 128]
        leads_ref[h] = lead_ref[:, h * 128 : (h + 1) * 128]
    fore = start_ref[...]
    back = end_ref[...]
    logs = jnp.zeros((chunks, 1), f32)
    spots = iota((chunks, 1), 0) * steps
    for k in range(steps):
        scaling = jnp.sum(fore * take(leads_ref, k, steps), axis=1, keepdims=True)
        scaled = take(split_ref, k, steps) * (exact / scaling)
        active = spots + k >= first
        fore = jnp.where(active, row_times(fore, ahead, states, 2) * scaled, fore)
        logs = logs + jnp.where(active, jnp.log(scaling), 0.0)
        put(fore_ref, k, steps, fore)
        j = steps - 1 - k
        put(back_ref, j, steps, back)
        weighed = back * take(split_ref, j, steps)
        inverse = exact / jnp.sum(weighed * sums, axis=1, keepdims=True)
        back = jnp.where(spots + j >= first, times_col(weighed, behind, states, 2) * inverse, back)
    joint = whole(fore_ref) * whole(back_ref)
    occupancy = jnp.where(iota((frames, 1), 0) >= first, normalize(joint), 0.0)
    occ_ref[...] = occupancy
    post_ref[...] = states * occupancy
    side = scal_ref[3]
    half = frames // 2
    keep_ref[...] = post_ref[pl.ds(pl.multiple_of(side * half, half), half), :]
    away_ref[...] = post_ref[pl.ds(pl.multiple_of((1 - side) * half, half), half), :]
    pack(pick_ref, meta_ref, occupancy, send_ref, scal_ref[2], jnp.sum(logs, axis=0, keepdims=True))


def counted(recv_ref, block):
    lines, states = recv_ref.shape
    counts = jnp.zeros((block, states), f32)
    totals = jnp.zeros((1, states), f32)
    slot = lax.bitwise_and(iota((block, states), 1), slots - 1)
    line = lax.bitwise_and(iota((states, states), 0), slots - 1)
    row = (iota((block, states), 0) + 1).astype(f32)
    metas = []
    for g in range(lines // states):
        came = recv_ref[g * states : (g + 1) * states, :]
        meta = jnp.sum(jnp.where(line == slots - 1, came, 0.0), axis=0, keepdims=True)
        totals = totals + jnp.sum(jnp.where(line == rows_sent, came, 0.0), axis=0, keepdims=True)
        pick = jnp.where((meta == row) & (slot < rows_sent), 1.0, 0.0).astype(bf16)
        high, mid, low = split3(came)
        counts = counts + (dot(pick, high) + (dot(pick, mid) + dot(pick, low)))
        metas.append(meta)
    return counts, totals, metas


def emit_update(counts, totals, total_rows):
    return total_rows * (counts + pseudo_count) / (totals + total_rows * pseudo_count)


def final_kernel(block, total_rows, emit_count, length, scal_ref, recv_ref, new_ref, log_ref,
                 counts_ref, totals_ref, most_ref):
    states = recv_ref.shape[1]
    counts, totals, metas = counted(recv_ref, block)
    counts_ref[...] = counts
    totals_ref[...] = totals
    new_ref[...] = emit_update(counts, totals, total_rows)
    lanes = iota((1, states), 1)
    slot = lax.bitwise_and(lanes, slots - 1)
    most = 0.0
    sums = [0.0, 0.0]
    for g, meta in enumerate(metas):
        most = jnp.maximum(most, jnp.max(jnp.where(slot == rows_sent + 1, meta, 0.0)))
        source = g * (states // slots) + lax.shift_right_logical(lanes, slots.bit_length() - 1)
        column = (lax.bitwise_and(source, emit_count - 1) == scal_ref[4]) & (slot == rows_sent)
        odd = lax.bitwise_and(lax.shift_right_logical(source, emit_count.bit_length() - 1), 1)
        for j in range(2):
            sums[j] = sums[j] + jnp.sum(jnp.where(column & (odd == j), meta, 0.0))
    most_ref[0] = most.astype(jnp.int32)
    for j in range(2):
        log_ref[j] = sums[j] / (length - scal_ref[5 + j]).astype(f32)


def posterior_kernel(scal_ref, keep_ref, other_ref, post_ref):
    side = scal_ref[3]
    post_ref[side] = keep_ref[...]
    post_ref[1 - side] = other_ref[...]


def pack_kernel(scal_ref, pick_ref, meta_ref, occ_ref, send_ref):
    pack(pick_ref, meta_ref, occ_ref[...], send_ref, scal_ref[2], 0.0)


def more_kernel(block, recv_ref, counts_ref, out_ref):
    counts, _, _ = counted(recv_ref, block)
    out_ref[...] = counts_ref[...] + counts


vmem = pl.BlockSpec(memory_space=pltpu.MemorySpace.VMEM)
smem = pl.BlockSpec(memory_space=pltpu.MemorySpace.SMEM)


def call(kernel, in_specs, out_specs, out_shape, scratch=(), cost=None, aliases=None):
    if cost is not None:
        cost = pl.CostEstimate(flops=cost, bytes_accessed=cost // 100, transcendentals=0)
    return pl.pallas_call(kernel, cost_estimate=cost,
                          input_output_aliases=aliases or {}, in_specs=in_specs, out_specs=out_specs, out_shape=out_shape,
                          scratch_shapes=scratch, compiler_params=pltpu.CompilerParams(vmem_limit_bytes=granted))


def shape(*dims, dtype=f32):
    return jax.ShapeDtypeStruct(dims, dtype)


def update(observed, starts, initial, transition, emission):
    traj_rows, frame_count = observed.shape
    states = transition.shape[0]
    tm_count = lax.axis_size("tm")
    emit_count = lax.axis_size("emit")
    emit_place = lax.axis_index("emit")
    both = ("tm", "emit")
    devices = tm_count * emit_count
    own_rows = emission.shape[0]
    total_rows = own_rows * emit_count
    block = total_rows // devices
    length = frame_count * tm_count
    assert traj_rows == 2 and tm_count % 2 == 0
    frames = 2 * frame_count
    parts = tm_count // 2

    ids = observed.reshape(1, frames)
    table = shape(own_rows, states, dtype=bf16)
    tables = call(table_kernel, [vmem], [vmem] * 3, [table] * 3, cost=400_000_000)(emission)
    scal = starts

    def placed(kernel, *fixed):
        def run(starts_ref, *refs):
            tm, emit = lax.axis_index("tm"), lax.axis_index("emit")
            odd, at = lax.rem(tm, 2), lax.div(tm, 2)
            base = lax.rem(tm * emit_count + emit, states // slots) * slots
            spot = (starts_ref[odd] - at * frames, at, base, odd, emit, starts_ref[0], starts_ref[1])
            kernel(*fixed, spot, *refs)

        return run

    def swaps(k):
        return [(i, i ^ k) for i in range(emit_count)]

    near = jnp.concatenate([ids, lax.ppermute(ids, "emit", swaps(1))], axis=0)
    far = [lax.ppermute(near, "emit", swaps(k)) for k in range(2, emit_count, 2)]
    far, tables = lax.optimization_barrier((far, tables))
    wanted = jnp.concatenate([near] + far, axis=0) - emit_place * own_rows
    gathered = shape(emit_count // 2, frames + 8, states)
    mine, other = call(gather_kernel, [vmem] * 4, [vmem, vmem], [gathered] * 2)(wanted, *tables)
    summed = mine + lax.ppermute(other, "emit", swaps(1))
    came, more = [], []
    for k in range(2, emit_count, 2):
        came.append(lax.ppermute(summed[k // 2, 0:frame_count], "emit", swaps(k)))
    taken = lax.ppermute(summed[0, frame_count:], "tm", [(i, i ^ 1) for i in range(tm_count)])
    for k in range(2, emit_count, 2):
        pairs = [(i, (i // emit_count ^ 1) * emit_count + (i % emit_count ^ k)) for i in range(devices)]
        more.append(lax.ppermute(summed[k // 2, frame_count:frames], both, pairs))
    narrow = shape(states, states, dtype=bf16)
    row = shape(1, states)
    refined = call(matrix_kernel, [vmem], [vmem] * 5, [narrow] * 3 + [row] * 2, cost=400_000_000)(transition)
    came, refined = lax.optimization_barrier((came, refined))
    matrices, exact, sums = refined[:3], refined[3], refined[4]
    nodes = 2 * chunks - 1
    count = len(came)

    early, late = placed(early_kernel, count), placed(late_kernel, count)
    mats = (transition, *matrices, exact, sums)
    leaves = shape(nodes, states, states, dtype=bf16)
    early_rows = shape(frame_count, states)
    scratch = [pltpu.VMEM((chunks, states), f32)] * 2 + [pltpu.VMEM((states, states), bf16)]
    early_w, early_lead, early_column, high, low = call(
        early, [smem] + [vmem] * (7 + count), [vmem] * 5, [early_rows, early_rows, row, leaves, leaves],
        scratch, cost=12_000_000_000,
    )(scal, summed, *came, *mats)
    weights, lead, high, low, state, message, root = call(
        late, [smem] + [vmem] * (13 + count), [vmem] * 7,
        [shape(frames, states), shape(frames, states), leaves, leaves, shape(8, states), shape(8, states),
         shape(states, states)],
        scratch + [pltpu.VMEM((frame_count, states), f32)] * 2, cost=12_000_000_000, aliases={12 + count: 2, 13 + count: 3},
    )(scal, taken, early_w, early_lead, early_column, initial.reshape(1, states), *more, *mats, high, low)

    def address(turn):
        kernel = placed(address_kernel, block, own_rows)
        lines = devices * slots
        return call(kernel, [smem, smem, vmem, vmem], [vmem, vmem],
                    [shape(lines, frames, dtype=bf16), shape(lines, states)], cost=400_000_000)(scal, turn, ids, taken)

    pick, meta = address(jnp.zeros((1,), jnp.int32))

    def relay_pairs(turn):
        pairs = []
        for y in range(2):
            pairs.append((2 * turn + y, 2 * turn + 2 + y))
            pairs.append((2 * (parts - 1 - turn) + y, 2 * (parts - 2 - turn) + y))
        return pairs

    def end_pairs(fore, back):
        return [pair for y in range(2) for pair in ((2 * fore + y, 2 * (parts - 1) + y), (2 * back + y, y))]

    assert parts >= 4
    recv = lax.ppermute(message, "tm", relay_pairs(0))
    edge = lax.ppermute(root, "tm", end_pairs(parts - 2, 1))
    for turn in range(1, parts - 2):
        relay = placed(relay_kernel, parts, turn)
        state, message = call(
            relay, [smem] + [vmem] * 4, [vmem] * 2, [shape(8, states), shape(8, states)]
        )(scal, state, recv, high, low)
        recv = lax.ppermute(message, "tm", relay_pairs(turn))
    ahead = lax.ppermute(message, "tm", end_pairs(parts - 3, 2))

    chain = placed(chain_kernel, parts)
    keep, away, occupancy, send = call(
        chain, [smem] + [vmem] * 14, [vmem] * 4,
        [shape(frame_count, states), shape(frame_count, states), shape(frames, states), shape(devices * slots, states)],
        [pltpu.VMEM((states // 128, frames, 128), f32)] * 4
        + [pltpu.VMEM((chunks, states), f32)] * 2 + [pltpu.VMEM((frames, states), f32)],
    )(scal, state, recv, ahead, edge, weights, lead, high, low, matrices[0], matrices[1], exact, sums, pick, meta)
    other = lax.ppermute(away, "tm", [(i, i ^ 1) for i in range(tm_count)])

    def exchange(sent):
        got = lax.all_to_all(sent.reshape(devices, slots, states), both, 0, 0, tiled=True)
        return got.reshape(devices * slots, states)

    final = placed(final_kernel, block, total_rows, emit_count, length)
    sent = exchange(send)
    posterior = call(placed(posterior_kernel), [smem, vmem, vmem], vmem, shape(2, frame_count, states),
                     cost=100_000_000)(scal, keep, other)
    new_emission, loglik, counts, totals, most = call(
        final, [smem, vmem], [vmem, smem, vmem, vmem, smem],
        [shape(block, states), shape(2), shape(block, states), shape(1, states), shape(1, dtype=jnp.int32)],
    )(scal, sent)

    def another(carried):
        turn, counts, _ = carried

        def more(*refs):
            more_kernel(block, *refs)

        sent = call(placed(pack_kernel), [smem] + [vmem] * 3, vmem, shape(devices * slots, states))(
            scal, *address(turn.reshape(1)), occupancy
        )
        counts = call(more, [vmem, vmem], vmem, shape(block, states))(exchange(sent), counts)
        return turn + 1, counts, emit_update(counts, totals, total_rows)

    _, _, new_emission = lax.while_loop(
        lambda carried: carried[0] * rows_sent < most[0], another, (jnp.int32(1), counts, new_emission)
    )
    return (posterior, new_emission, loglik)


def solution(mesh):
    in_specs = (P("emit", "tm"), P("emit"), P(), P(), P("emit", None))
    out_specs = (P("emit", "tm", None), P(("tm", "emit"), None), P("emit"))
    return jax.shard_map(update, mesh=mesh, in_specs=in_specs, out_specs=out_specs, check_vma=False)
```
